256 devices in a mesh: tx: 32 (over y, z_hi, core), ty: 8 (over x, z_lo).
Axes of the slice: x: 4, y: 4, z: 8 (z_hi: 4, z_lo: 2; z = z_hi * 2 + z_lo), core: 2. Of those that a mesh axis runs over, the one named last changes fastest.
Arguments:
- cells: bfloat16 [32, 8, 512, 512], P('tx', 'ty'), may hold values from -6 to 6
- halo_inputs: bfloat16 [32, 8, 256, 512], P('tx', 'ty'), may hold values from -6 to 6
- stale_halo: bfloat16 [32, 8, 1, 256, 512], P('tx', 'ty'), may hold values from -6 to 6
- stale_returned: bfloat16 [32, 8, 1, 256, 512], P('tx', 'ty'), may hold values from -3 to 3
- cotangent: bfloat16 [32, 8, 512, 512], P('tx', 'ty'), may hold values from -6 to 6
- expression: bfloat16 [32, 8, 512, 512], P('tx', 'ty'), may hold values from -6 to 6
- halo_expression: bfloat16 [32, 8, 256, 512], P('tx', 'ty'), may hold values from -6 to 6
- neighbours: int32 [32, 8, 16, 512], P('tx', 'ty'), may hold values from 0 to 767
- edge_mask: int32 [32, 8, 16, 512], P('tx', 'ty'), may hold values 0 or 1
- send_rows: int32 [32, 8, 8, 32], P('tx', 'ty'), may hold values from 0 to 511
- live_cells: int32 [32, 8], P('tx', 'ty'), may hold values from 256 to 512
- ligand_genes: int32 [1024], replicated, may hold values from 0 to 511
- receptor_genes: int32 [1024], replicated, may hold values from 0 to 511
- gate_weights: float32 [1024], replicated, may hold values from -0.1875 to 0.1875
- self_weights: bfloat16 [2, 512, 512], replicated, may hold values from -0.25 to 0.25
- neighbour_weights: bfloat16 [2, 512, 512], replicated, may hold values from -0.25 to 0.25
Outputs:
- fresh_halo: bfloat16 [32, 8, 1, 256, 512], P('tx', 'ty')
- returned_grads: bfloat16 [32, 8, 1, 256, 512], P('tx', 'ty')
- layer_updates: float32 [4, 512, 512], replicated
- gate_update: float32 [1024], replicated
The draws below stay inside these ranges and needn't reach their ends.
All inputs are finite; a program needn't handle non-finite values. No bound on the sum of `edge_mask` on one device may be relied on, other than what follows from the above.
Results may differ from the reference program's by a relative error of at most 0.0062.
Values may be sent and summed in bfloat16 or wider, within the bound.
No kernel may reach another device: no remote copies, remote signals or barrier semaphores. Data moves between devices by JAX's collectives and lax.ppermute only.
A program may use at most 64 MiB of HBM per device.

```python
import jax
import jax.numpy as jnp
from jax import lax

WIDTH = 512
PAIRS = 1024
GENES = 512
DEGREE = 16
LAYERS = 2
CELLS = 512
BORDER = 32
HALO = 256
N_TX = 32
N_TY = 8


def plant(entries, stream_key, smallest, high):
    shape = entries.shape
    place = [jax.random.randint(jax.random.fold_in(stream_key, axis), (), 0, shape[axis]) for axis in range(len(shape))]
    entries = entries.at[tuple(place)].set(smallest)
    longest = shape.index(max(shape))
    place[longest] = (place[longest] + 1) % shape[longest]
    return entries.at[tuple(place)].set(high)


def level_of(rng, dims, shards, least, high):
    def one(axis_at, parts):
        steps = jax.random.uniform(jax.random.fold_in(jax.random.fold_in(rng, 6), axis_at), (parts,), jnp.float32, least / len(shards), high / len(shards))
        return jnp.repeat(jnp.exp(steps), dims[axis_at] // parts).reshape((-1,) + (1,) * (len(dims) - axis_at - 1))

    factor_of = one(*shards[0])
    for cut in shards[1:]:
        factor_of = factor_of * one(*cut)
    return factor_of


def normal_values(key, dims, deviation, reach, split=(), kind=jnp.bfloat16):
    result = jax.random.normal(key, dims, jnp.float32) * deviation
    if len(split) > 0:
        result = level_of(key, dims, split, -0.22, 0.18) * result
    return jnp.clip(result, min=-reach, max=reach).astype(kind)


def setup_inputs(seed: int = 0) -> dict:
    streams_of = jax.random.split(jax.random.key(seed), 17)
    cells = normal_values(streams_of[0], (N_TX, N_TY, CELLS, WIDTH), 1.0, 6.0, ((0, 32), (1, 8)))
    halo_inputs = normal_values(streams_of[1], (N_TX, N_TY, HALO, WIDTH), 1.0, 6.0, ((0, 32), (1, 8)))
    stale_halo = normal_values(streams_of[2], (N_TX, N_TY, LAYERS - 1, HALO, WIDTH), 1.0, 6.0, ((0, 32), (1, 8)))
    stale_returned = normal_values(streams_of[3], (N_TX, N_TY, LAYERS - 1, HALO, WIDTH), 0.5, 3.0, ((0, 32), (1, 8)))
    cotangent = normal_values(streams_of[4], (N_TX, N_TY, CELLS, WIDTH), 1.0, 6.0, ((0, 32), (1, 8)))
    expression = normal_values(streams_of[5], (N_TX, N_TY, CELLS, GENES), 1.0, 6.0, ((0, 32), (1, 8)))
    halo_expression = normal_values(streams_of[6], (N_TX, N_TY, HALO, GENES), 1.0, 6.0, ((0, 32), (1, 8)))
    neighbours = plant(jax.random.randint(streams_of[7], (N_TX, N_TY, DEGREE, CELLS), 0, CELLS + HALO), jax.random.fold_in(streams_of[7], 1), 0, (CELLS + HALO) - 1).astype(jnp.int32)
    edge_mask = plant((jax.random.randint(streams_of[8], (N_TX, N_TY, DEGREE, CELLS), 0, 4) < 3).astype(jnp.int32), jax.random.fold_in(streams_of[8], 1), 0, 1)
    send_rows = plant(jax.random.randint(streams_of[9], (N_TX, N_TY, 8, BORDER), 0, CELLS), jax.random.fold_in(streams_of[9], 1), 0, CELLS - 1).astype(jnp.int32)
    live_cells = plant(jax.random.randint(streams_of[10], (N_TX, N_TY), CELLS // 2, CELLS + 1), jax.random.fold_in(streams_of[10], 1), CELLS // 2, CELLS).astype(jnp.int32)
    ligand_genes = plant(jax.random.randint(streams_of[11], (PAIRS,), 0, GENES), jax.random.fold_in(streams_of[11], 1), 0, GENES - 1).astype(jnp.int32)
    receptor_genes = plant(jax.random.randint(streams_of[12], (PAIRS,), 0, GENES), jax.random.fold_in(streams_of[12], 1), 0, GENES - 1).astype(jnp.int32)
    gate_weights = normal_values(streams_of[13], (PAIRS,), PAIRS ** -0.5, 0.1875, (), jnp.float32)
    self_weights = normal_values(streams_of[14], (LAYERS, WIDTH, WIDTH), WIDTH ** -0.5, 0.25)
    neighbour_weights = normal_values(streams_of[15], (LAYERS, WIDTH, WIDTH), WIDTH ** -0.5, 0.25)
    return {"cells": cells, "halo_inputs": halo_inputs, "stale_halo": stale_halo, "stale_returned": stale_returned, "cotangent": cotangent, "expression": expression, "halo_expression": halo_expression, "neighbours": neighbours, "edge_mask": edge_mask, "send_rows": send_rows, "live_cells": live_cells, "ligand_genes": ligand_genes, "receptor_genes": receptor_genes, "gate_weights": gate_weights, "self_weights": self_weights, "neighbour_weights": neighbour_weights}


OFFSETS = ((-1, -1), (-1, 0), (-1, 1), (0, -1), (0, 1), (1, -1), (1, 0), (1, 1))

def silu_slope(pre_act):
    sigmoid_value = jax.nn.sigmoid(pre_act)
    return sigmoid_value * (1.0 + pre_act * (1.0 - sigmoid_value))

def tile_pass(tile_data, ligand_genes, receptor_genes, gate_weights, self_weights, neighbour_weights):
    own_state, halo_first, stale_rows, stale_back, upstream, genes_here, genes_halo, neighbour_ids, valid_edges, outgoing, live_count = tile_data
    cell_count = own_state.shape[0]
    model_width = own_state.shape[1]
    ligand = jnp.concatenate([genes_here, genes_halo], 0)[:, ligand_genes]
    receptor = genes_here[:, receptor_genes]
    scaled = receptor.astype(jnp.float32) * gate_weights[None, :]
    picked = ligand[neighbour_ids].astype(jnp.float32)
    edge_score = lax.optimization_barrier(jnp.sum(picked * scaled[None], axis=-1))
    gate_value = jax.nn.sigmoid(edge_score)
    weight = 0.25 * valid_edges.astype(jnp.float32) * gate_value
    states = [own_state]
    full_rows = []
    aggregates = []
    pre_acts = []
    for layer_id in range(LAYERS):
        halo_rows = halo_first if layer_id == 0 else stale_rows[layer_id - 1]
        joined = jnp.concatenate([states[layer_id], halo_rows], 0)
        gathered = joined[neighbour_ids].astype(jnp.float32)
        aggregate = lax.optimization_barrier(jnp.sum(weight[:, :, None] * gathered, axis=0)).astype(jnp.bfloat16)
        pre_act = jnp.dot(states[layer_id], self_weights[layer_id], preferred_element_type=jnp.float32)
        pre_act = pre_act + jnp.dot(aggregate, neighbour_weights[layer_id], preferred_element_type=jnp.float32)
        full_rows.append(joined)
        aggregates.append(aggregate)
        pre_acts.append(pre_act)
        if layer_id + 1 < LAYERS:
            states.append((states[layer_id].astype(jnp.float32) + jax.nn.silu(pre_act)).astype(jnp.bfloat16))
    live_rows = (jnp.arange(cell_count) < live_count)[:, None]
    grad_state = jnp.where(live_rows, upstream.astype(jnp.float32), jnp.float32(0.0))
    edge_grad = jnp.zeros(neighbour_ids.shape, jnp.float32)
    layer_grads = [None] * (2 * LAYERS)
    halo_grads = []
    for layer_id in range(LAYERS - 1, -1, -1):
        grad_pre = (grad_state * silu_slope(pre_acts[layer_id])).astype(jnp.bfloat16)
        layer_grads[2 * layer_id] = jnp.dot(states[layer_id].T, grad_pre, preferred_element_type=jnp.float32)
        layer_grads[2 * layer_id + 1] = jnp.dot(aggregates[layer_id].T, grad_pre, preferred_element_type=jnp.float32)
        grad_aggregate = jnp.dot(grad_pre, neighbour_weights[layer_id].T, preferred_element_type=jnp.float32).astype(jnp.bfloat16)
        wide_grad = grad_aggregate.astype(jnp.float32)
        gathered = full_rows[layer_id][neighbour_ids].astype(jnp.float32)
        edge_grad = edge_grad + lax.optimization_barrier(jnp.sum(gathered * wide_grad[None], axis=-1))
        if layer_id > 0:
            spread = (weight[:, :, None] * wide_grad[None]).reshape(-1, model_width)
            grad_full = jnp.zeros((full_rows[layer_id].shape[0], model_width), jnp.float32)
            grad_full = grad_full.at[neighbour_ids.reshape(-1)].add(spread)
            halo_grads.insert(0, grad_full[cell_count:].astype(jnp.bfloat16).reshape(8, -1, model_width))
            grad_state = grad_state + jnp.dot(grad_pre, self_weights[layer_id].T, preferred_element_type=jnp.float32)
            grad_state = grad_state + grad_full[:cell_count]
            grad_state = grad_state.at[outgoing.reshape(-1)].add(stale_back[layer_id - 1].astype(jnp.float32))
    grad_score = 0.25 * valid_edges.astype(jnp.float32) * edge_grad * gate_value * (1.0 - gate_value)
    gate_grad = lax.optimization_barrier(jnp.sum(lax.optimization_barrier(jnp.sum(grad_score[:, :, None] * picked, axis=0)) * receptor.astype(jnp.float32), axis=0))
    send_blocks = jnp.stack([states[layer_id][outgoing] for layer_id in range(1, LAYERS)])
    return (send_blocks, jnp.stack(halo_grads), jnp.stack(layer_grads), gate_grad)

def move_blocks(blocks, direction_sign):
    widths = ((1, 1), (1, 1)) + ((0, 0),) * (blocks.ndim - 2)
    padded = jnp.pad(blocks, widths)
    moved_list = []
    for direction, (delta_x, delta_y) in enumerate(OFFSETS):
        start_x = 1 - direction_sign * delta_x
        start_y = 1 - direction_sign * delta_y
        moved_list.append(padded[start_x:start_x + N_TX, start_y:start_y + N_TY, :, direction])
    return jnp.stack(moved_list, axis=3)

def reference(cells, halo_inputs, stale_halo, stale_returned, cotangent, expression, halo_expression, neighbours, edge_mask, send_rows, live_cells, ligand_genes, receptor_genes, gate_weights, self_weights, neighbour_weights):
    tile_count = N_TX * N_TY
    model_width = cells.shape[-1]
    per_tile = tuple((value.reshape((tile_count,) + value.shape[2:]) for value in (cells, halo_inputs, stale_halo, stale_returned, cotangent, expression, halo_expression, neighbours, edge_mask, send_rows, live_cells)))

    def tile_step(running, tile_data):
        send_blocks, halo_grads, layer_grads, gate_grad = tile_pass(tile_data, ligand_genes, receptor_genes, gate_weights, self_weights, neighbour_weights)
        return ((running[0] + layer_grads, running[1] + gate_grad), (send_blocks, halo_grads))
    initial = (jnp.zeros((2 * LAYERS, model_width, model_width), jnp.float32), jnp.zeros((PAIRS,), jnp.float32))
    (layer_sum, gate_sum), (send_all, halo_all) = lax.scan(tile_step, initial, per_tile)
    grid_shape = (N_TX, N_TY) + send_all.shape[1:]
    fresh_blocks = move_blocks(send_all.reshape(grid_shape), 1)
    returned_blocks = move_blocks(halo_all.reshape(grid_shape), -1)
    halo_shape = (N_TX, N_TY, LAYERS - 1, -1, model_width)
    square = jnp.sum(layer_sum * layer_sum) + jnp.sum(gate_sum * gate_sum)
    clip_factor = jnp.minimum(1.0, 2.0 * model_width / jnp.sqrt(square + 1e-06))
    return (fresh_blocks.reshape(halo_shape), returned_blocks.reshape(halo_shape), clip_factor * layer_sum, clip_factor * gate_sum)
```

```python
import functools

import jax
import jax.numpy as jnp
from jax import lax
from jax.experimental import pallas as pl
from jax.experimental.pallas import tpu as pltpu
from jax.sharding import PartitionSpec as P

F32 = jnp.float32
BF16 = jnp.bfloat16
AXES = ("tx", "ty")


def ring_label(position):
    return position ^ (position >> 1)


def place(index):
    tx, ty = divmod(index, 8)
    y, z_hi, core = tx // 8, (tx // 2) % 4, tx % 2
    x, z_lo = ty // 2, ty % 2
    return x, y, z_hi * 2 + z_lo, core


def index_of(x, y, z, core):
    return (y * 8 + (z // 2) * 2 + core) * 8 + x * 2 + z % 2


def unlabel(label):
    return label ^ (label >> 1)


def xor_pairs(kind, flip):
    pairs = []
    for index in range(256):
        x, y, z, core = place(index)
        if kind == "core":
            core ^= 1
        elif kind == "z":
            label = (z ^ (z >> 1)) ^ flip
            z = label ^ (label >> 1) ^ (label >> 2)
        else:
            along_x = (kind == "first") == (core == 0)
            if along_x:
                x = unlabel(ring_label(x) ^ flip)
            else:
                y = unlabel(ring_label(y) ^ flip)
        pairs.append((index, index_of(x, y, z, core)))
    return pairs


def swap(value, kind, flip=1):
    return lax.ppermute(value, AXES, xor_pairs(kind, flip))


def nn(a, b):
    return lax.dot_general(a, b, (((1,), (0,)), ((), ())), preferred_element_type=F32)


def nt(a, b):
    return lax.dot_general(a, b, (((1,), (1,)), ((), ())), preferred_element_type=F32)


def tn(a, b):
    return lax.dot_general(a, b, (((0,), (0,)), ((), ())), preferred_element_type=F32)


def tile_kernel(
    place_ref, nbr, msk, snd, lig, rec, gwt,
    cells, halo, stale, sback, cot, expr, hexpr, ws, wn,
    o_lm, o_lp, o_mm, o_mp, o_keep, o_send, o_gate,
    full0, full1, xall, sb, ct, wsv, wnv, cnt, adj, slope_g, inner, slope0, agg0, grads, sems,
):
    n, w = ct.shape
    full_n = full0.shape[0]

    def fetch(src, dst, slot):
        copy = pltpu.make_async_copy(src, dst, sems.at[slot])
        copy.start()
        return copy

    c_expr = fetch(expr, xall.at[pl.ds(0, n)], 0)
    c_hexpr = fetch(hexpr, xall.at[pl.ds(n, full_n - n)], 1)
    c_cells = fetch(cells, full0.at[pl.ds(0, n)], 2)
    c_halo = fetch(halo, full0.at[pl.ds(n, full_n - n)], 3)
    c_ws = fetch(ws, wsv, 4)
    c_wn = fetch(wn, wnv, 5)
    c_stale = fetch(stale, full1.at[pl.ds(n, full_n - n)], 6)
    c_cot = fetch(cot, ct, 7)
    c_sb = fetch(sback, sb, 8)

    ids = nbr[...]
    low = jnp.bitwise_and(ids, 127)
    field = jnp.left_shift(msk[...], 5 * jnp.right_shift(ids, 7))
    rows128 = lax.broadcasted_iota(jnp.int32, (128, 128), 0)
    for part in range(n // 128):
        cols = slice(part * 128, part * 128 + 128)
        words = jnp.zeros((128, 128), jnp.int32)
        for k in range(ids.shape[0]):
            words = words + jnp.where(rows128 == low[k : k + 1, cols], field[k : k + 1, cols], 0)
        words = words.T
        for block in range(full_n // 128):
            count = jnp.bitwise_and(jnp.right_shift(words, 5 * block), 31)
            cnt[cols, block * 128 : block * 128 + 128] = (0.25 * count.astype(F32)).astype(BF16)

    genes = xall.shape[1]
    pairs = lig.shape[1]
    gene_rows = lax.broadcasted_iota(jnp.int32, (genes, pairs), 0)
    rec_table = jnp.where(gene_rows == rec[...], gwt[...], 0.0).astype(BF16)
    lig_table = jnp.where(gene_rows == lig[...], 1.0, 0.0).astype(BF16)
    mixed = nt(rec_table, lig_table).astype(BF16)
    c_expr.wait()
    c_hexpr.wait()
    left = nn(xall[0:n], mixed).astype(BF16)
    half_tanh = 0.5 * jnp.tanh(0.5 * nt(left, xall[...]))
    count = cnt[...].astype(F32)
    weight = count * (0.5 + half_tanh)
    adj[...] = weight.astype(BF16)
    slope_g[...] = weight * (0.5 - half_tanh)

    c_cells.wait()
    c_halo.wait()
    state0 = full0[0:n]
    agg0[...] = nn(adj[...], full0[...]).astype(BF16)
    c_ws.wait()
    c_wn.wait()
    pre0 = nn(state0, wsv[0]) + nn(agg0[...], wnv[0])
    sig0 = 0.5 + 0.5 * jnp.tanh(0.5 * pre0)
    slope0[...] = sig0 * (1.0 + pre0 * (1.0 - sig0))
    full1[0:n] = (state0.astype(F32) + pre0 * sig0).astype(BF16)

    c_stale.wait()
    agg1 = nn(adj[...], full1[...]).astype(BF16)
    pre1 = nn(full1[0:n], wsv[1]) + nn(agg1, wnv[1])
    sig1 = 0.5 + 0.5 * jnp.tanh(0.5 * pre1)
    slope1 = sig1 * (1.0 + pre1 * (1.0 - sig1))
    c_cot.wait()
    live = lax.broadcasted_iota(jnp.int32, (n, w), 0) < place_ref[0]
    carried = jnp.where(live, ct[...].astype(F32), 0.0)
    gpre1 = (carried * slope1).astype(BF16)
    grads[2 * n : 3 * n] = tn(full1[0:n], gpre1)
    grads[3 * n : 4 * n] = tn(agg1, gpre1)
    gagg1 = nt(gpre1, wnv[1]).astype(BF16)
    inner[...] = nt(gagg1, full1[...])
    gfull = tn(adj[...], gagg1)
    back = gfull[n:].astype(BF16)

    sent = snd.shape[1]
    send_table = jnp.where(
        lax.broadcasted_iota(jnp.int32, (n, sent), 0) == snd[...], 1.0, 0.0
    ).astype(BF16)
    fresh = tn(send_table, full1[0:n]).astype(BF16)
    b = sent // 8
    o_lm[0] = fresh[0 : 3 * b]
    o_lp[0] = fresh[5 * b : 8 * b]
    o_mm[0] = fresh[3 * b : 4 * b]
    o_mp[0] = fresh[4 * b : 5 * b]
    for pos in range(3):
        o_lm[1, pos * b : (pos + 1) * b] = back[(7 - pos) * b : (8 - pos) * b]
        o_lp[1, pos * b : (pos + 1) * b] = back[(2 - pos) * b : (3 - pos) * b]
    o_mm[1] = back[4 * b : 5 * b]
    o_mp[1] = back[3 * b : 4 * b]

    c_sb.wait()
    carried = carried + nt(gpre1, wsv[1]) + gfull[:n] + nn(send_table, sb[...])
    gpre0 = (carried * slope0[...]).astype(BF16)
    grads[0:n] = tn(state0, gpre0)
    grads[n : 2 * n] = tn(agg0[...], gpre0)
    gagg0 = nt(gpre0, wnv[0]).astype(BF16)
    spread = (slope_g[...] * (inner[...] + nt(gagg0, full0[...]))).astype(BF16)
    gathered = nn(spread, xall[...]).astype(BF16)
    gene_grad = tn(xall[0:n], gathered)
    gene_hi = gene_grad.astype(BF16)
    gene_lo = (gene_grad - gene_hi.astype(F32)).astype(BF16)
    by_pair = nn(gene_hi, lig_table) + nn(gene_lo, lig_table)
    gate = jnp.sum(jnp.where(gene_rows == rec[...], by_pair, 0.0), axis=0, keepdims=True)
    gate8 = jnp.concatenate(
        [gate[:, :w], gate[:, w:], jnp.zeros((6, w), F32)], axis=0
    )
    gate_hi = gate8.astype(BF16)
    gate_lo = (gate8 - gate_hi.astype(F32)).astype(BF16)
    o_gate[...] = gate_hi.astype(F32) + gate_lo.astype(F32)

    core = place_ref[1]
    half = 2 * n
    step = half // 16
    for j in range(16):
        here = pl.multiple_of(core * half + (place_ref[2] ^ j) * step, step)
        there = pl.multiple_of((1 - core) * half + (place_ref[3] ^ j) * step, step)
        o_keep[j * step : (j + 1) * step] = grads[pl.ds(here, step)]
        o_send[j * step : (j + 1) * step] = grads[pl.ds(there, step)].astype(BF16)
    o_send[half:] = jnp.concatenate([gate_hi.astype(F32), gate_lo.astype(F32)], 0).astype(BF16)


def sum_kernel(counts, *refs):
    arrivals, split = counts
    own, gate = refs[0], refs[1]
    got = refs[2 : 2 + arrivals]
    outs = refs[2 + arrivals :]
    rows = own.shape[0]

    def gate_of(ref):
        both = ref[rows : rows + 16].astype(F32)
        return both[0:8] + both[8:16]

    def total(lo, hi):
        value = own[lo:hi]
        for ref in got:
            value = value + ref[lo:hi].astype(F32)
        return value

    if arrivals == 3:
        gates = (gate[...] + gate_of(got[2])) + (gate_of(got[0]) + gate_of(got[1]))
    else:
        gates = gate[...] + gate_of(got[0])
    gate_hi = gates.astype(BF16).astype(F32)
    gate_lo = (gates - gate_hi).astype(BF16).astype(F32)
    if split:
        part = rows // 4
        keep, gate_out, sends = outs[0], outs[1], outs[2:]
        keep[...] = total(0, part)
        gate_out[...] = gate_hi + gate_lo
        for j, ref in enumerate(sends, 1):
            ref[0:part] = total(j * part, (j + 1) * part).astype(BF16)
            ref[part:] = jnp.concatenate([gate_hi, gate_lo], 0).astype(BF16)
    else:
        outs[0][0:rows] = total(0, rows)
        outs[0][rows:] = gates


def add_kernel(a, b, o):
    o[...] = a[...] + b[...]


def last_kernel(place_ref, own, other, gate_own, gate_other, o_layers, o_gate, whole):
    rows, w = own.shape
    core = place_ref[1]
    step = rows // 16
    total = jnp.zeros((8, w), F32)
    for j in range(16):
        here = pl.multiple_of(core * rows + (place_ref[2] ^ j) * step, step)
        there = pl.multiple_of((1 - core) * rows + (place_ref[3] ^ j) * step, step)
        whole[pl.ds(here, step)] = own[j * step : (j + 1) * step].astype(F32)
        whole[pl.ds(there, step)] = other[j * step : (j + 1) * step].astype(F32)
    gate = jnp.where(core == 0, gate_own[...], gate_other[...])
    total = total + gate * gate
    for j in range(32):
        part = whole[j * step : (j + 1) * step]
        square = part * part
        for k in range(step // 8):
            total = total + square[k * 8 : (k + 1) * 8]
    square = jnp.sum(jnp.sum(total, axis=0, keepdims=True), axis=1, keepdims=True)
    clip = jnp.minimum(1.0, (2.0 * w) / jnp.sqrt(square + 1e-06))
    o_layers[...] = whole[...] * clip
    o_gate[...] = gate * clip


def call(kernel, outs, *args, scratch=(), smem=0):
    specs = [pl.BlockSpec(memory_space=pltpu.SMEM)] * smem
    specs += [pl.BlockSpec(memory_space=pltpu.VMEM)] * (len(args) - smem)
    return pl.pallas_call(
        kernel,
        out_shape=outs,
        in_specs=specs,
        out_specs=jax.tree.map(lambda _: pl.BlockSpec(memory_space=pltpu.VMEM), outs),
        scratch_shapes=list(scratch),
        compiler_params=pltpu.CompilerParams(vmem_limit_bytes=48 * 1024 * 1024),
    )(*args)


def shape(rows, w, kind):
    return jax.ShapeDtypeStruct((rows, w), kind)


def from_behind(value, axis, steps):
    count = lax.axis_size(axis)
    first, last = (max(0, -steps), min(count, count - steps))
    return lax.ppermute(value, axis, [(source, source + steps) for source in range(first, last)])


def on_device(
    cells, halo_inputs, stale_halo, stale_returned, cotangent, expression, halo_expression,
    neighbours, edge_mask, send_rows, live_cells, ligand_genes, receptor_genes, gate_weights,
    self_weights, neighbour_weights,
):
    n, w = cells.shape[2:]
    h = halo_inputs.shape[2]
    degree = neighbours.shape[2]
    pairs = ligand_genes.shape[0]
    genes = expression.shape[3]
    b = h // 8

    tx, ty = lax.axis_index("tx"), lax.axis_index("ty")
    x_label, y_label, core = ring_label(ty // 2), ring_label(tx // 8), tx % 2
    x_first, y_first = x_label * 4 + y_label, y_label * 4 + x_label
    mine = jnp.where(core == 0, x_first, y_first)
    partner = jnp.where(core == 0, y_first, x_first)
    where = jnp.stack([live_cells[0, 0], core, mine, partner]).astype(jnp.int32)

    vmem = pl.BlockSpec(memory_space=pltpu.VMEM)
    hbm = pl.BlockSpec(memory_space=pl.ANY)
    outs = (
        jax.ShapeDtypeStruct((2, 3 * b, w), BF16),
        jax.ShapeDtypeStruct((2, 3 * b, w), BF16),
        jax.ShapeDtypeStruct((2, b, w), BF16),
        jax.ShapeDtypeStruct((2, b, w), BF16),
        shape(2 * n, w, F32),
        shape(2 * n + 16, w, BF16),
        shape(8, w, F32),
    )
    lead_m, lead_p, mid_m, mid_p, keep, send, gate = pl.pallas_call(
        tile_kernel,
        out_shape=outs,
        in_specs=[pl.BlockSpec(memory_space=pltpu.SMEM)] + [vmem] * 6 + [hbm] * 9,
        out_specs=(vmem,) * len(outs),
        scratch_shapes=[
            pltpu.VMEM((n + h, w), BF16),
            pltpu.VMEM((n + h, w), BF16),
            pltpu.VMEM((n + h, genes), BF16),
            pltpu.VMEM((h, w), BF16),
            pltpu.VMEM((n, w), BF16),
            pltpu.VMEM((2, w, w), BF16),
            pltpu.VMEM((2, w, w), BF16),
            pltpu.VMEM((n, n + h), BF16),
            pltpu.VMEM((n, n + h), BF16),
            pltpu.VMEM((n, n + h), F32),
            pltpu.VMEM((n, n + h), F32),
            pltpu.VMEM((n, w), F32),
            pltpu.VMEM((n, w), BF16),
            pltpu.VMEM((4 * n, w), F32),
            pltpu.SemaphoreType.DMA((9,)),
        ],
        compiler_params=pltpu.CompilerParams(vmem_limit_bytes=56 * 1024 * 1024),
    )(
        where,
        neighbours.reshape(degree, n),
        edge_mask.reshape(degree, n),
        send_rows.reshape(1, h),
        ligand_genes.reshape(1, pairs),
        receptor_genes.reshape(1, pairs),
        gate_weights.reshape(1, pairs),
        cells.reshape(n, w),
        halo_inputs.reshape(h, w),
        stale_halo.reshape(h, w),
        stale_returned.reshape(h, w),
        cotangent.reshape(n, w),
        expression.reshape(n, genes),
        halo_expression.reshape(h, genes),
        self_weights,
        neighbour_weights,
    )

    got = swap(send, "core")
    part = n // 2
    quarter = [shape(part, w, F32), shape(8, w, F32)] + [shape(part + 16, w, BF16)] * 3
    keep, gate, *sends = call(functools.partial(sum_kernel, (1, True)), quarter, keep, gate, got)
    got = [swap(value, "first", j) for j, value in enumerate(sends, 1)]
    part = part // 4
    quarter = [shape(part, w, F32), shape(8, w, F32)] + [shape(part + 16, w, BF16)] * 3
    keep, gate, *sends = call(functools.partial(sum_kernel, (3, True)), quarter, keep, gate, *got)
    got = [swap(value, "second", j) for j, value in enumerate(sends, 1)]
    both = call(
        functools.partial(sum_kernel, (3, False)), shape(part + 8, w, F32), keep, gate, *got
    )
    for flip in (1, 2, 4):
        both = both + swap(both, "z", flip)
    own, gate = both[:part].astype(BF16), both[part:]
    own = jnp.concatenate([own] + [swap(own, "second", j) for j in (1, 2, 3)], 0)
    own = jnp.concatenate([own] + [swap(own, "first", j) for j in (1, 2, 3)], 0)
    other = swap(own, "core")
    gate_other = swap(gate, "core")

    lead_m = from_behind(lead_m, "tx", -1).reshape(2, 3, b, w)
    lead_p = from_behind(lead_p, "tx", 1).reshape(2, 3, b, w)
    cross_m = jnp.stack([mid_m, lead_m[:, 0], lead_p[:, 0]], 1)
    cross_p = jnp.stack([mid_p, lead_m[:, 2], lead_p[:, 2]], 1)
    cross_m = from_behind(cross_m, "ty", -1)
    cross_p = from_behind(cross_p, "ty", 1)
    arrived = [
        cross_m[:, 1], lead_m[:, 1], cross_p[:, 1], cross_m[:, 0],
        cross_p[:, 0], cross_m[:, 2], lead_p[:, 1], cross_p[:, 2],
    ]
    fresh = jnp.concatenate([value[0] for value in arrived], 0)
    returned = jnp.concatenate([value[1] for value in arrived[::-1]], 0)

    layers, gate = call(
        last_kernel, (shape(4 * n, w, F32), shape(8, w, F32)), where, own, other, gate, gate_other,
        scratch=[pltpu.VMEM((4 * n, w), F32)], smem=1,
    )
    halo_shape = (1, 1, 1, h, w)
    return (
        fresh.reshape(halo_shape),
        returned.reshape(halo_shape),
        layers.reshape(4, n, w),
        gate[:2].reshape(pairs),
    )


def solution(mesh):
    tile = P("tx", "ty")
    return jax.shard_map(
        on_device,
        mesh=mesh,
        in_specs=(tile,) * 11 + (P(),) * 5,
        out_specs=(tile, tile, P(), P()),
        check_vma=False,
    )
```

```python
import jax
import jax.numpy as jnp
from jax import lax
from jax.experimental import pallas as pl
from jax.experimental.pallas import tpu as pltpu
from jax.sharding import PartitionSpec as P

F32 = jnp.float32
BF16 = jnp.bfloat16
AXES = ("tx", "ty")


def ring_label(position):
    return position ^ (position >> 1)


def place(index):
    tx, ty = divmod(index, 8)
    y, z_hi, core = tx // 8, (tx // 2) % 4, tx % 2
    x, z_lo = ty // 2, ty % 2
    return x, y, z_hi * 2 + z_lo, core


def index_of(x, y, z, core):
    return (y * 8 + (z // 2) * 2 + core) * 8 + x * 2 + z % 2


def unlabel(label):
    return label ^ (label >> 1)


def xor_pairs(kind, flip):
    pairs = []
    for index in range(256):
        x, y, z, core = place(index)
        if kind == "core":
            core ^= 1
        elif kind == "z":
            label = (z ^ (z >> 1)) ^ flip
            z = label ^ (label >> 1) ^ (label >> 2)
        else:
            bit = core if kind == "first" else 1 - core
            x = unlabel(ring_label(x) ^ ((flip & 1) << bit))
            y = unlabel(ring_label(y) ^ ((flip >> 1) << bit))
        pairs.append((index, index_of(x, y, z, core)))
    return pairs


def swap(value, kind, flip=1):
    return lax.ppermute(value, AXES, xor_pairs(kind, flip))


def nn(a, b):
    return lax.dot_general(a, b, (((1,), (0,)), ((), ())), preferred_element_type=F32)


def nt(a, b):
    return lax.dot_general(a, b, (((1,), (1,)), ((), ())), preferred_element_type=F32)


def tn(a, b):
    return lax.dot_general(a, b, (((0,), (0,)), ((), ())), preferred_element_type=F32)


def my_labels():
    tx, ty = lax.axis_index("tx"), lax.axis_index("ty")
    x, y, core = ring_label(ty // 2), ring_label(tx // 8), tx % 2
    low = 2 * (y & 1) + (x & 1)
    high = 2 * (y >> 1) + (x >> 1)
    low_first, high_first = 4 * low + high, 4 * high + low
    mine = jnp.where(core == 0, low_first, high_first)
    partner = jnp.where(core == 0, high_first, low_first)
    return core, mine, partner


def put_gate(ref, row, gate):
    hi = gate.astype(BF16).astype(F32)
    lo = (gate - hi).astype(BF16).astype(F32)
    ref[row : row + 16, 0:128] = jnp.concatenate([hi, lo], 0).astype(BF16)
    return hi + lo


def get_gate(ref, row):
    both = ref[row : row + 16, 0:128].astype(F32)
    return both[0:8] + both[8:16]


def tile_kernel(
    live_ref, nbr_in, msk_in, snd_in, lig_in, rec_in, gwt_in,
    cells, halo, stale, sback, cot, expr, hexpr, ws, wn,
    o_lm, o_lp, o_mm, o_mp, o_keep, o_send, o_gate,
    full0, full1, xall, sb, ct, wsv, wnv, cnt, adj, slope_g, inner, slope0, agg0, grads,
    nbr, msk, snd, lig, rec, gwt, sems,
):
    n, w = ct.shape
    full_n = full0.shape[0]

    def fetch(src, dst, slot):
        copy = pltpu.make_async_copy(src, dst, sems.at[slot])
        copy.start()
        return copy

    small = (
        (nbr_in, nbr), (msk_in, msk), (lig_in, lig), (rec_in, rec), (gwt_in, gwt), (snd_in, snd),
    )
    c_small = [fetch(src, dst, 9 + k) for k, (src, dst) in enumerate(small)]
    c_expr = fetch(expr, xall.at[pl.ds(0, n)], 0)
    c_hexpr = fetch(hexpr, xall.at[pl.ds(n, full_n - n)], 1)
    c_cells = fetch(cells, full0.at[pl.ds(0, n)], 2)
    c_halo = fetch(halo, full0.at[pl.ds(n, full_n - n)], 3)
    c_ws = fetch(ws, wsv, 4)
    c_wn = fetch(wn, wnv, 5)
    c_stale = fetch(stale, full1.at[pl.ds(n, full_n - n)], 6)
    c_cot = fetch(cot, ct, 7)
    c_sb = fetch(sback, sb, 8)

    for copy in c_small:
        copy.wait()
    ids = nbr[...]
    low = jnp.bitwise_and(ids, 127)
    field = jnp.left_shift(msk[...], 5 * jnp.right_shift(ids, 7))
    rows128 = lax.broadcasted_iota(jnp.int32, (128, 128), 0)
    for part in range(n // 128):
        cols = slice(part * 128, part * 128 + 128)
        words = jnp.zeros((128, 128), jnp.int32)
        for k in range(ids.shape[0]):
            words = words + jnp.where(rows128 == low[k : k + 1, cols], field[k : k + 1, cols], 0)
        words = words.T
        for block in range(full_n // 128):
            count = jnp.bitwise_and(jnp.right_shift(words, 5 * block), 31)
            cnt[cols, block * 128 : block * 128 + 128] = (0.25 * count.astype(F32)).astype(BF16)

    genes = xall.shape[1]
    pairs = lig.shape[1]
    gene_rows = lax.broadcasted_iota(jnp.int32, (genes, pairs), 0)
    rec_table = jnp.where(gene_rows == rec[...], gwt[...], 0.0).astype(BF16)
    lig_table = jnp.where(gene_rows == lig[...], 1.0, 0.0).astype(BF16)
    mixed = nt(rec_table, lig_table).astype(BF16)
    c_expr.wait()
    c_hexpr.wait()
    left = nn(xall[0:n], mixed).astype(BF16)
    half_tanh = 0.5 * jnp.tanh(0.5 * nt(left, xall[...]))
    count = cnt[...].astype(F32)
    weight = count * (0.5 + half_tanh)
    adj[...] = weight.astype(BF16)
    slope_g[...] = weight * (0.5 - half_tanh)

    c_cells.wait()
    c_halo.wait()
    state0 = full0[0:n]
    agg0[...] = nn(adj[...], full0[...]).astype(BF16)
    c_ws.wait()
    c_wn.wait()
    pre0 = nn(state0, wsv[0]) + nn(agg0[...], wnv[0])
    sig0 = 0.5 + 0.5 * jnp.tanh(0.5 * pre0)
    slope0[...] = sig0 * (1.0 + pre0 * (1.0 - sig0))
    full1[0:n] = (state0.astype(F32) + pre0 * sig0).astype(BF16)

    c_stale.wait()
    agg1 = nn(adj[...], full1[...]).astype(BF16)
    pre1 = nn(full1[0:n], wsv[1]) + nn(agg1, wnv[1])
    sig1 = 0.5 + 0.5 * jnp.tanh(0.5 * pre1)
    slope1 = sig1 * (1.0 + pre1 * (1.0 - sig1))
    c_cot.wait()
    live = lax.broadcasted_iota(jnp.int32, (n, w), 0) < live_ref[0, 0]
    carried = jnp.where(live, ct[...].astype(F32), 0.0)
    gpre1 = (carried * slope1).astype(BF16)
    grads[2 * n : 3 * n] = tn(full1[0:n], gpre1)
    grads[3 * n : 4 * n] = tn(agg1, gpre1)
    gagg1 = nt(gpre1, wnv[1]).astype(BF16)
    inner[...] = nt(gagg1, full1[...])
    gfull = tn(adj[...], gagg1)
    back = gfull[n:].astype(BF16)

    send_ids = jnp.concatenate([snd[d : d + 1] for d in range(8)], axis=1)
    sent = send_ids.shape[1]
    send_table = jnp.where(
        lax.broadcasted_iota(jnp.int32, (n, sent), 0) == send_ids, 1.0, 0.0
    ).astype(BF16)
    fresh = tn(send_table, full1[0:n]).astype(BF16)
    b = sent // 8
    o_lm[0] = fresh[0 : 3 * b]
    o_lp[0] = fresh[5 * b : 8 * b]
    o_mm[0] = fresh[3 * b : 4 * b]
    o_mp[0] = fresh[4 * b : 5 * b]
    for pos in range(3):
        o_lm[1, pos * b : (pos + 1) * b] = back[(7 - pos) * b : (8 - pos) * b]
        o_lp[1, pos * b : (pos + 1) * b] = back[(2 - pos) * b : (3 - pos) * b]
    o_mm[1] = back[4 * b : 5 * b]
    o_mp[1] = back[3 * b : 4 * b]

    c_sb.wait()
    carried = carried + nt(gpre1, wsv[1]) + gfull[:n] + nn(send_table, sb[...])
    gpre0 = (carried * slope0[...]).astype(BF16)
    grads[0:n] = tn(state0, gpre0)
    grads[n : 2 * n] = tn(agg0[...], gpre0)
    gagg0 = nt(gpre0, wnv[0]).astype(BF16)
    spread = (slope_g[...] * (inner[...] + nt(gagg0, full0[...]))).astype(BF16)
    gathered = nn(spread, xall[...]).astype(BF16)
    gene_grad = tn(xall[0:n], gathered)
    gene_hi = gene_grad.astype(BF16)
    gene_lo = (gene_grad - gene_hi.astype(F32)).astype(BF16)
    by_pair = nn(gene_hi, lig_table) + nn(gene_lo, lig_table)
    gate = jnp.sum(jnp.where(gene_rows == rec[...], by_pair, 0.0), axis=0, keepdims=True)
    gate = jnp.concatenate([gate[:, k * 128 : k * 128 + 128] for k in range(8)], axis=0)

    core, mine, partner = my_labels()
    half = 2 * n
    step = half // 16
    for j in range(16):
        here = pl.multiple_of(core * half + (mine ^ j) * step, step)
        there = pl.multiple_of((1 - core) * half + (partner ^ j) * step, step)
        o_keep[j * step : (j + 1) * step] = grads[pl.ds(here, step)]
        o_send[j * step : (j + 1) * step] = grads[pl.ds(there, step)].astype(BF16)
    o_gate[...] = put_gate(o_send, half, gate)


def split_four(total, gates, rows, keep, gate_out, sends):
    part = rows // 4
    keep[...] = total(0, part)
    for j, ref in enumerate(sends, 1):
        ref[0:part] = total(j * part, (j + 1) * part).astype(BF16)
        kept = put_gate(ref, part, gates)
    gate_out[...] = kept


def after_core(own, gate, got, lead_m, lead_p, keep, gate_out, s1, s2, s3, o_lm, o_lp):
    rows = own.shape[0]
    split_four(
        lambda lo, hi: own[lo:hi] + got[lo:hi].astype(F32),
        gate[...] + get_gate(got, rows),
        rows, keep, gate_out, (s1, s2, s3),
    )
    o_lm[...] = lead_m[...]
    o_lp[...] = lead_p[...]


def four(own, got):
    def total(lo, hi):
        return (own[lo:hi] + got[2][lo:hi].astype(F32)) + (
            got[0][lo:hi].astype(F32) + got[1][lo:hi].astype(F32)
        )

    return total


def four_gates(gate, got, rows):
    return (gate[...] + get_gate(got[2], rows)) + (get_gate(got[0], rows) + get_gate(got[1], rows))


def after_first(
    own, gate, r1, r2, r3, lead_m, lead_p, mid_m, mid_p,
    keep, gate_out, s1, s2, s3, cross_m, cross_p,
):
    rows = own.shape[0]
    got = (r1, r2, r3)
    split_four(four(own, got), four_gates(gate, got, rows), rows, keep, gate_out, (s1, s2, s3))
    b = mid_m.shape[1]
    for k in range(2):
        for ref, mid, cut in ((cross_m, mid_m, 0), (cross_p, mid_p, 2)):
            ref[k, 0:b] = mid[k]
            ref[k, b : 2 * b] = lead_m[k, cut * b : (cut + 1) * b]
            ref[k, 2 * b : 3 * b] = lead_p[k, cut * b : (cut + 1) * b]


def after_second(own, gate, r1, r2, r3, out):
    rows = own.shape[0]
    got = (r1, r2, r3)
    out[0:rows] = four(own, got)(0, rows)
    out[rows:, 0:128] = four_gates(gate, got, rows)


def add_wide(a, b, out):
    rows = out.shape[0] - 16
    out[0:rows] = (a[0:rows] + b[0:rows]).astype(BF16)
    put_gate(out, rows, a[rows:, 0:128] + b[rows:, 0:128])


def add_narrow(a, b, out):
    rows = out.shape[0] - 16
    out[0:rows] = (a[0:rows].astype(F32) + b[0:rows].astype(F32)).astype(BF16)
    put_gate(out, rows, get_gate(a, rows) + get_gate(b, rows))


def add_last(a, b, own, gate):
    rows = own.shape[0]
    own[...] = (a[0:rows].astype(F32) + b[0:rows].astype(F32)).astype(BF16)
    put_gate(gate, 0, get_gate(a, rows) + get_gate(b, rows))


def join(*refs):
    out, row = refs[-1], 0
    for ref in refs[:-1]:
        out[row : row + ref.shape[0]] = ref[...]
        row += ref.shape[0]


def join_through(own, r1, r2, r3, gate, cross_m, cross_p, out, o_cross_m, o_cross_p):
    join(own, r1, r2, r3, gate, out)
    o_cross_m[...] = cross_m[...]
    o_cross_p[...] = cross_p[...]


def squares(ref, label):
    rows, w = ref.shape[0] - 16, ref.shape[1]
    step = rows // 16
    total = jnp.zeros((8, w), F32)
    for j in range(16):
        part = ref[pl.ds(pl.multiple_of((label ^ j) * step, step), step)].astype(F32)
        part = part * part
        for k in range(step // 8):
            total = total + part[k * 8 : (k + 1) * 8]
    return total


def own_squares(own, lead_m, lead_p, cross_m, cross_p, o_squares, o_fresh, o_returned):
    _, mine, _ = my_labels()
    o_squares[...] = squares(own, mine)
    b = o_fresh.shape[0] // 8
    arrived = (
        (cross_m, 1), (lead_m, 1), (cross_p, 1), (cross_m, 0),
        (cross_p, 0), (cross_m, 2), (lead_p, 1), (cross_p, 2),
    )
    for d, (ref, cut) in enumerate(arrived):
        o_fresh[d * b : (d + 1) * b] = ref[0, cut * b : (cut + 1) * b]
        o_returned[(7 - d) * b : (8 - d) * b] = ref[1, cut * b : (cut + 1) * b]


def last_kernel(own, other, own_sq, o_layers, o_gate, whole, sems):
    rows, w = own.shape[0] - 16, own.shape[1]
    core, mine, partner = my_labels()
    step = rows // 16
    other_sq = squares(other, partner)
    gate = jnp.where(core == 0, get_gate(own, rows), get_gate(other, rows))
    total = jnp.sum(own_sq[...] + other_sq, axis=0, keepdims=True)
    square = jnp.sum(total, axis=1, keepdims=True)
    square = square + jnp.sum(
        jnp.sum(gate * gate, axis=0, keepdims=True), axis=1, keepdims=True
    )
    clip = jnp.minimum(1.0, (2.0 * w) / jnp.sqrt(square + 1e-06))
    o_gate[...] = gate * clip
    copies = []
    for side, (ref, label, which) in enumerate(((own, mine, core), (other, partner, 1 - core))):
        for group in range(4):
            slot = side * 4 + group
            for j in range(4 * group, 4 * group + 4):
                row = pl.multiple_of((label ^ j) * step, step)
                part = ref[pl.ds(row, step)].astype(F32) * clip
                whole[side * rows + j * step : side * rows + (j + 1) * step] = part
            target = pl.multiple_of(which * rows + group * 4 * step, step)
            copy = pltpu.make_async_copy(
                whole.at[pl.ds(side * rows + group * 4 * step, 4 * step)],
                o_layers.at[pl.ds(target, 4 * step)],
                sems.at[slot],
            )
            copy.start()
            copies.append(copy)
    for copy in copies:
        copy.wait()


def call(kernel, outs, *args, scratch=(), hbm_outs=0):
    vmem, hbm = pl.BlockSpec(memory_space=pltpu.VMEM), pl.BlockSpec(memory_space=pl.ANY)
    return pl.pallas_call(
        kernel,
        out_shape=outs,
        in_specs=[vmem] * len(args),
        out_specs=(hbm,) * hbm_outs + (vmem,) * (len(outs) - hbm_outs),
        scratch_shapes=list(scratch),
        compiler_params=pltpu.CompilerParams(vmem_limit_bytes=16 * 1024 * 1024),
    )(*args)


def shape(rows, w, kind):
    return jax.ShapeDtypeStruct((rows, w), kind)


def from_behind(value, axis, steps):
    count = lax.axis_size(axis)
    first, last = (max(0, -steps), min(count, count - steps))
    return lax.ppermute(value, axis, [(source, source + steps) for source in range(first, last)])


def on_device(
    cells, halo_inputs, stale_halo, stale_returned, cotangent, expression, halo_expression,
    neighbours, edge_mask, send_rows, live_cells, ligand_genes, receptor_genes, gate_weights,
    self_weights, neighbour_weights,
):
    n, w = cells.shape[2:]
    h = halo_inputs.shape[2]
    degree = neighbours.shape[2]
    pairs = ligand_genes.shape[0]
    genes = expression.shape[3]
    b = h // 8

    vmem = pl.BlockSpec(memory_space=pltpu.VMEM)
    hbm = pl.BlockSpec(memory_space=pltpu.HBM)
    outs = (
        jax.ShapeDtypeStruct((2, 3 * b, w), BF16),
        jax.ShapeDtypeStruct((2, 3 * b, w), BF16),
        jax.ShapeDtypeStruct((2, b, w), BF16),
        jax.ShapeDtypeStruct((2, b, w), BF16),
        shape(2 * n, w, F32),
        shape(2 * n + 16, w, BF16),
        shape(8, 128, F32),
    )
    lead_m, lead_p, mid_m, mid_p, keep, send, gate = pl.pallas_call(
        tile_kernel,
        out_shape=outs,
        in_specs=[pl.BlockSpec(memory_space=pltpu.SMEM)] + [hbm] * 15,
        out_specs=(vmem,) * len(outs),
        scratch_shapes=[
            pltpu.VMEM((n + h, w), BF16),
            pltpu.VMEM((n + h, w), BF16),
            pltpu.VMEM((n + h, genes), BF16),
            pltpu.VMEM((h, w), BF16),
            pltpu.VMEM((n, w), BF16),
            pltpu.VMEM((2, w, w), BF16),
            pltpu.VMEM((2, w, w), BF16),
            pltpu.VMEM((n, n + h), BF16),
            pltpu.VMEM((n, n + h), BF16),
            pltpu.VMEM((n, n + h), F32),
            pltpu.VMEM((n, n + h), F32),
            pltpu.VMEM((n, w), F32),
            pltpu.VMEM((n, w), BF16),
            pltpu.VMEM((4 * n, w), F32),
            pltpu.VMEM((degree, n), jnp.int32),
            pltpu.VMEM((degree, n), jnp.int32),
            pltpu.VMEM((8, b), jnp.int32),
            pltpu.VMEM((1, pairs), jnp.int32),
            pltpu.VMEM((1, pairs), jnp.int32),
            pltpu.VMEM((1, pairs), F32),
            pltpu.SemaphoreType.DMA((15,)),
        ],
        compiler_params=pltpu.CompilerParams(vmem_limit_bytes=40 * 1024 * 1024),
    )(
        live_cells,
        *(
            pltpu.with_memory_space_constraint(value, pltpu.HBM)
            for value in (
                neighbours.reshape(degree, n),
                edge_mask.reshape(degree, n),
                send_rows.reshape(8, b),
                ligand_genes.reshape(1, pairs),
                receptor_genes.reshape(1, pairs),
                gate_weights.reshape(1, pairs),
                cells.reshape(n, w),
                halo_inputs.reshape(h, w),
                stale_halo.reshape(h, w),
                stale_returned.reshape(h, w),
                cotangent.reshape(n, w),
                expression.reshape(n, genes),
                halo_expression.reshape(h, genes),
                self_weights,
                neighbour_weights,
            )
        ),
    )

    def quarter(part):
        return (shape(part, w, F32), shape(8, 128, F32)) + (shape(part + 16, w, BF16),) * 3

    wide = jax.ShapeDtypeStruct((2, 3 * b, w), BF16)
    got = swap(send, "core")
    part = n // 2
    keep, gate, s1, s2, s3, lead_m, lead_p = call(
        after_core, quarter(part) + (wide, wide), keep, gate, got, lead_m, lead_p
    )
    got = [swap(value, "first", j) for j, value in ((1, s1), (2, s2), (3, s3))]
    lead_m = from_behind(lead_m, "tx", -1)
    lead_p = from_behind(lead_p, "tx", 1)
    part = part // 4
    keep, gate, s1, s2, s3, cross_m, cross_p = call(
        after_first, quarter(part) + (wide, wide), keep, gate, *got, lead_m, lead_p, mid_m, mid_p
    )
    got = [swap(value, "second", j) for j, value in ((1, s1), (2, s2), (3, s3))]
    (both,) = call(after_second, (shape(part + 8, w, F32),), keep, gate, *got)
    (both,) = call(add_wide, (shape(part + 16, w, BF16),), both, swap(both, "z", 1))
    (both,) = call(add_narrow, (shape(part + 16, w, BF16),), both, swap(both, "z", 2))
    own, gate = call(
        add_last, (shape(part, w, BF16), shape(16, w, BF16)), both, swap(both, "z", 4)
    )
    got = [swap(own, "second", j) for j in (1, 2, 3)]
    (own,) = call(join, (shape(4 * part, w, BF16),), own, *got)
    got = [swap(own, "first", j) for j in (1, 2, 3)]
    cross_m = from_behind(cross_m, "ty", -1)
    cross_p = from_behind(cross_p, "ty", 1)
    own, cross_m, cross_p = call(
        join_through, (shape(16 * part + 16, w, BF16), wide, wide), own, *got, gate, cross_m, cross_p
    )
    other = swap(own, "core")
    own_sq, fresh, returned = call(
        own_squares, (shape(8, w, F32), shape(h, w, BF16), shape(h, w, BF16)),
        own, lead_m, lead_p, cross_m, cross_p,
    )
    layers, gate = call(
        last_kernel, (shape(4 * n, w, F32), shape(8, 128, F32)), own, other, own_sq,
        scratch=[pltpu.VMEM((4 * n, w), F32), pltpu.SemaphoreType.DMA((8,))], hbm_outs=1,
    )
    halo_shape = (1, 1, 1, h, w)
    return (
        fresh.reshape(halo_shape),
        returned.reshape(halo_shape),
        layers.reshape(4, n, w),
        gate.reshape(pairs),
    )


def solution(mesh):
    tile = P("tx", "ty")
    return jax.shard_map(
        on_device,
        mesh=mesh,
        in_specs=(tile,) * 11 + (P(),) * 5,
        out_specs=(tile, tile, P(), P()),
        check_vma=False,
    )
```

```python
import jax
import jax.numpy as jnp
from jax import lax
from jax.experimental import pallas as pl
from jax.experimental.pallas import tpu as pltpu
from jax.sharding import PartitionSpec as P


F32 = jnp.float32
BF16 = jnp.bfloat16
AXES = ("tx", "ty")


def ring_label(position):
    return position ^ (position >> 1)


def place(index):
    tx, ty = divmod(index, 8)
    y, z_hi, core = tx // 8, (tx // 2) % 4, tx % 2
    x, z_lo = ty // 2, ty % 2
    return x, y, z_hi * 2 + z_lo, core


def index_of(x, y, z, core):
    return (y * 8 + (z // 2) * 2 + core) * 8 + x * 2 + z % 2


def unlabel(label):
    return label ^ (label >> 1)


def xor_pairs(kind, flip):
    pairs = []
    for index in range(256):
        x, y, z, core = place(index)
        if kind == "core":
            core ^= 1
        elif kind == "z":
            label = (z ^ (z >> 1)) ^ (1, 2, 4)[(flip + core) % 3]
            z = label ^ (label >> 1) ^ (label >> 2)
        else:
            bit = core if kind == "first" else 1 - core
            x = unlabel(ring_label(x) ^ ((flip & 1) << bit))
            y = unlabel(ring_label(y) ^ ((flip >> 1) << bit))
        pairs.append((index, index_of(x, y, z, core)))
    return pairs


def swap(value, kind, flip=1):
    return lax.ppermute(value, AXES, xor_pairs(kind, flip))


def nn(a, b):
    return lax.dot_general(a, b, (((1,), (0,)), ((), ())), preferred_element_type=F32)


def nt(a, b):
    return lax.dot_general(a, b, (((1,), (1,)), ((), ())), preferred_element_type=F32)


def tn(a, b):
    return lax.dot_general(a, b, (((0,), (0,)), ((), ())), preferred_element_type=F32)


def my_labels():
    tx, ty = lax.axis_index("tx"), lax.axis_index("ty")
    x, y, core = ring_label(ty // 2), ring_label(tx // 8), tx % 2
    low = 2 * (y & 1) + (x & 1)
    high = 2 * (y >> 1) + (x >> 1)
    low_first, high_first = 4 * low + high, 4 * high + low
    mine = jnp.where(core == 0, low_first, high_first)
    partner = jnp.where(core == 0, high_first, low_first)
    return core, mine, partner


def put_gate(ref, row, gate):
    hi = gate.astype(BF16).astype(F32)
    lo = (gate - hi).astype(BF16).astype(F32)
    ref[row : row + 16, 0:128] = jnp.concatenate([hi, lo], 0).astype(BF16)
    return hi + lo


def get_gate(ref, row):
    both = ref[row : row + 16, 0:128].astype(F32)
    return both[0:8] + both[8:16]


def tile_kernel(
    live_ref, nbr_in, msk_in, snd_in, lig_in, rec_in, gwt_in,
    cells, halo, stale, sback, cot, expr, hexpr, ws, wn,
    o_lm, o_lp, o_mm, o_mp, o_keep, o_send, o_gate,
    full0, full1, xall, sb, ct, wsv, wnv, cnt, adj, slope_g, inner, slope0, agg0, grads,
    nbr, msk, snd, lig, rec, gwt, sems,
):
    n, w = ct.shape
    full_n = full0.shape[0]

    def fetch(src, dst, slot):
        copy = pltpu.make_async_copy(src, dst, sems.at[slot])
        copy.start()
        return copy

    small = (
        (nbr_in, nbr), (msk_in, msk), (lig_in, lig), (rec_in, rec), (gwt_in, gwt), (snd_in, snd),
    )
    c_small = [fetch(src, dst, 9 + k) for k, (src, dst) in enumerate(small)]
    c_expr = fetch(expr, xall.at[pl.ds(0, n)], 0)
    c_hexpr = fetch(hexpr, xall.at[pl.ds(n, full_n - n)], 1)
    c_cells = fetch(cells, full0.at[pl.ds(0, n)], 2)
    c_halo = fetch(halo, full0.at[pl.ds(n, full_n - n)], 3)
    c_ws = fetch(ws, wsv, 4)
    c_wn = fetch(wn, wnv, 5)
    c_stale = fetch(stale, full1.at[pl.ds(n, full_n - n)], 6)
    c_cot = fetch(cot, ct, 7)
    c_sb = fetch(sback, sb, 8)

    for copy in c_small:
        copy.wait()
    ids = nbr[...]
    low = jnp.bitwise_and(ids, 127)
    field = jnp.left_shift(msk[...], 5 * jnp.right_shift(ids, 7))
    rows128 = lax.broadcasted_iota(jnp.int32, (128, 128), 0)
    for part in range(n // 128):
        cols = slice(part * 128, part * 128 + 128)
        words = jnp.zeros((128, 128), jnp.int32)
        for k in range(ids.shape[0]):
            words = words + jnp.where(rows128 == low[k : k + 1, cols], field[k : k + 1, cols], 0)
        words = words.T
        for block in range(full_n // 128):
            count = jnp.bitwise_and(jnp.right_shift(words, 5 * block), 31)
            cnt[cols, block * 128 : block * 128 + 128] = (0.25 * count.astype(F32)).astype(BF16)

    genes = xall.shape[1]
    pairs = lig.shape[1]
    gene_rows = lax.broadcasted_iota(jnp.int32, (genes, pairs), 0)
    rec_table = jnp.where(gene_rows == rec[...], gwt[...], 0.0).astype(BF16)
    lig_table = jnp.where(gene_rows == lig[...], 1.0, 0.0).astype(BF16)
    mixed = nt(rec_table, lig_table).astype(BF16)
    c_expr.wait()
    c_hexpr.wait()
    left = nn(xall[0:n], mixed).astype(BF16)
    half_tanh = 0.5 * jnp.tanh(0.5 * nt(left, xall[...]))
    count = cnt[...].astype(F32)
    weight = count * (0.5 + half_tanh)
    adj[...] = weight.astype(BF16)
    slope_g[...] = weight * (0.5 - half_tanh)

    c_cells.wait()
    c_halo.wait()
    state0 = full0[0:n]
    agg0[...] = nn(adj[...], full0[...]).astype(BF16)
    c_ws.wait()
    c_wn.wait()
    pre0 = nn(state0, wsv[0]) + nn(agg0[...], wnv[0])
    sig0 = 0.5 + 0.5 * jnp.tanh(0.5 * pre0)
    slope0[...] = sig0 * (1.0 + pre0 * (1.0 - sig0))
    full1[0:n] = (state0.astype(F32) + pre0 * sig0).astype(BF16)

    c_stale.wait()
    agg1 = nn(adj[...], full1[...]).astype(BF16)
    pre1 = nn(full1[0:n], wsv[1]) + nn(agg1, wnv[1])
    sig1 = 0.5 + 0.5 * jnp.tanh(0.5 * pre1)
    slope1 = sig1 * (1.0 + pre1 * (1.0 - sig1))
    c_cot.wait()
    live = lax.broadcasted_iota(jnp.int32, (n, w), 0) < live_ref[0, 0]
    carried = jnp.where(live, ct[...].astype(F32), 0.0)
    gpre1 = (carried * slope1).astype(BF16)
    grads[2 * n : 3 * n] = tn(full1[0:n], gpre1)
    grads[3 * n : 4 * n] = tn(agg1, gpre1)
    gagg1 = nt(gpre1, wnv[1]).astype(BF16)
    inner[...] = nt(gagg1, full1[...])
    gfull = tn(adj[...], gagg1)
    back = gfull[n:].astype(BF16)

    send_ids = jnp.concatenate([snd[d : d + 1] for d in range(8)], axis=1)
    sent = send_ids.shape[1]
    send_table = jnp.where(
        lax.broadcasted_iota(jnp.int32, (n, sent), 0) == send_ids, 1.0, 0.0
    ).astype(BF16)
    fresh = tn(send_table, full1[0:n]).astype(BF16)
    b = sent // 8
    o_lm[0] = fresh[0 : 3 * b]
    o_lp[0] = fresh[5 * b : 8 * b]
    o_mm[0] = fresh[3 * b : 4 * b]
    o_mp[0] = fresh[4 * b : 5 * b]
    for pos in range(3):
        o_lm[1, pos * b : (pos + 1) * b] = back[(7 - pos) * b : (8 - pos) * b]
        o_lp[1, pos * b : (pos + 1) * b] = back[(2 - pos) * b : (3 - pos) * b]
    o_mm[1] = back[4 * b : 5 * b]
    o_mp[1] = back[3 * b : 4 * b]

    c_sb.wait()
    carried = carried + nt(gpre1, wsv[1]) + gfull[:n] + nn(send_table, sb[...])
    gpre0 = (carried * slope0[...]).astype(BF16)
    grads[0:n] = tn(state0, gpre0)
    grads[n : 2 * n] = tn(agg0[...], gpre0)
    gagg0 = nt(gpre0, wnv[0]).astype(BF16)
    spread = (slope_g[...] * (inner[...] + nt(gagg0, full0[...]))).astype(BF16)
    gathered = nn(spread, xall[...]).astype(BF16)
    gene_grad = tn(xall[0:n], gathered)
    gene_hi = gene_grad.astype(BF16)
    gene_lo = (gene_grad - gene_hi.astype(F32)).astype(BF16)
    by_pair = nn(gene_hi, lig_table) + nn(gene_lo, lig_table)
    gate = jnp.sum(jnp.where(gene_rows == rec[...], by_pair, 0.0), axis=0, keepdims=True)
    gate = jnp.concatenate([gate[:, k * 128 : k * 128 + 128] for k in range(8)], axis=0)

    core, mine, partner = my_labels()
    half = 2 * n
    step = half // 16
    for j in range(16):
        here = pl.multiple_of(core * half + (mine ^ j) * step, step)
        there = pl.multiple_of((1 - core) * half + (partner ^ j) * step, step)
        o_keep[j * step : (j + 1) * step] = grads[pl.ds(here, step)]
        o_send[j * step : (j + 1) * step] = grads[pl.ds(there, step)].astype(BF16)
    o_gate[...] = put_gate(o_send, half, gate)


def split_four(total, gates, rows, keep, gate_out, sends):
    part = rows // 4
    keep[...] = total(0, part)
    for j, ref in enumerate(sends, 1):
        ref[0:part] = total(j * part, (j + 1) * part).astype(BF16)
        kept = put_gate(ref, part, gates)
    gate_out[...] = kept


def put_valid(dst, src, valid):
    @pl.when(valid)
    def _():
        dst[...] = src[...]

    @pl.when(jnp.logical_not(valid))
    def _():
        dst[...] = jnp.zeros(dst.shape, dst.dtype)


def has_after(axis):
    return lax.axis_index(axis) < lax.axis_size(axis) - 1


def has_before(axis):
    return lax.axis_index(axis) > 0


def after_core(own, gate, got, keep, gate_out, s1, s2, s3):
    rows = own.shape[0]
    split_four(
        lambda lo, hi: own[lo:hi] + got[lo:hi].astype(F32),
        gate[...] + get_gate(got, rows),
        rows, keep, gate_out, (s1, s2, s3),
    )


def four(own, got):
    def total(lo, hi):
        return (own[lo:hi] + got[2][lo:hi].astype(F32)) + (
            got[0][lo:hi].astype(F32) + got[1][lo:hi].astype(F32)
        )

    return total


def four_gates(gate, got, rows):
    return (gate[...] + get_gate(got[2], rows)) + (get_gate(got[0], rows) + get_gate(got[1], rows))


def after_first(
    own, gate, r1, r2, r3, lead_m, lead_p, mid_m, mid_p,
    keep, gate_out, s1, s2, s3, cross_m, cross_p,
):
    rows = own.shape[0]
    got = (r1, r2, r3)
    split_four(four(own, got), four_gates(gate, got, rows), rows, keep, gate_out, (s1, s2, s3))
    b = mid_m.shape[1]
    for k in range(2):
        for ref, mid, cut in ((cross_m, mid_m, 0), (cross_p, mid_p, 2)):
            ref[k, 0:b] = mid[k]
            rows = pl.ds(cut * b, b)
            put_valid(ref.at[k, pl.ds(b, b)], lead_m.at[k, rows], has_after("tx"))
            put_valid(ref.at[k, pl.ds(2 * b, b)], lead_p.at[k, rows], has_before("tx"))


def after_second(own, gate, r1, r2, r3, out):
    rows = own.shape[0]
    got = (r1, r2, r3)
    out[0:rows] = four(own, got)(0, rows)
    out[rows:, 0:128] = four_gates(gate, got, rows)


def add_wide(a, b, out):
    rows = out.shape[0] - 16
    out[0:rows] = (a[0:rows] + b[0:rows]).astype(BF16)
    put_gate(out, rows, a[rows:, 0:128] + b[rows:, 0:128])


def add_narrow(a, b, out):
    rows = out.shape[0] - 16
    out[0:rows] = (a[0:rows].astype(F32) + b[0:rows].astype(F32)).astype(BF16)
    put_gate(out, rows, get_gate(a, rows) + get_gate(b, rows))


def add_last(a, b, own, gate):
    rows = own.shape[0]
    own[...] = (a[0:rows].astype(F32) + b[0:rows].astype(F32)).astype(BF16)
    put_gate(gate, 0, get_gate(a, rows) + get_gate(b, rows))


def join(*refs):
    out, row = refs[-1], 0
    for ref in refs[:-1]:
        out[row : row + ref.shape[0]] = ref[...]
        row += ref.shape[0]


def squares(ref, label):
    rows, w = ref.shape[0] - 16, ref.shape[1]
    step = rows // 16
    total = jnp.zeros((8, w), F32)
    for j in range(16):
        part = ref[pl.ds(pl.multiple_of((label ^ j) * step, step), step)].astype(F32)
        part = part * part
        for k in range(step // 8):
            total = total + part[k * 8 : (k + 1) * 8]
    return total


def own_squares(own, lead_m, lead_p, cross_m, cross_p, o_squares, o_fresh, o_returned):
    _, mine, _ = my_labels()
    o_squares[...] = squares(own, mine)
    b = o_fresh.shape[0] // 8
    l_m, l_p = (lead_m, has_after("tx")), (lead_p, has_before("tx"))
    c_m, c_p = (cross_m, has_after("ty")), (cross_p, has_before("ty"))
    arrived = (
        (c_m, 1), (l_m, 1), (c_p, 1), (c_m, 0), (c_p, 0), (c_m, 2), (l_p, 1), (c_p, 2),
    )
    for d, ((ref, valid), cut) in enumerate(arrived):
        rows = pl.ds(cut * b, b)
        put_valid(o_fresh.at[pl.ds(d * b, b)], ref.at[0, rows], valid)
        put_valid(o_returned.at[pl.ds((7 - d) * b, b)], ref.at[1, rows], valid)


def last_kernel(own, other, own_sq, o_layers, o_gate, whole, sems):
    rows, w = own.shape[0] - 16, own.shape[1]
    core, mine, partner = my_labels()
    step = rows // 16
    other_sq = squares(other, partner)
    gate = jnp.where(core == 0, get_gate(own, rows), get_gate(other, rows))
    total = jnp.sum(own_sq[...] + other_sq, axis=0, keepdims=True)
    square = jnp.sum(total, axis=1, keepdims=True)
    square = square + jnp.sum(
        jnp.sum(gate * gate, axis=0, keepdims=True), axis=1, keepdims=True
    )
    clip = jnp.minimum(1.0, (2.0 * w) / jnp.sqrt(square + 1e-06))
    o_gate[...] = gate * clip
    copies = []
    for side, (ref, label, which) in enumerate(((own, mine, core), (other, partner, 1 - core))):
        for group in range(4):
            slot = side * 4 + group
            for j in range(4 * group, 4 * group + 4):
                row = pl.multiple_of((label ^ j) * step, step)
                part = ref[pl.ds(row, step)].astype(F32) * clip
                whole[side * rows + j * step : side * rows + (j + 1) * step] = part
            target = pl.multiple_of(which * rows + group * 4 * step, step)
            copy = pltpu.make_async_copy(
                whole.at[pl.ds(side * rows + group * 4 * step, 4 * step)],
                o_layers.at[pl.ds(target, 4 * step)],
                sems.at[slot],
            )
            copy.start()
            copies.append(copy)
    for copy in copies:
        copy.wait()


def call(kernel, outs, *args, scratch=(), hbm_outs=0):
    vmem, hbm = pl.BlockSpec(memory_space=pltpu.VMEM), pl.BlockSpec(memory_space=pl.ANY)
    return pl.pallas_call(
        kernel,
        out_shape=outs,
        in_specs=[vmem] * len(args),
        out_specs=(hbm,) * hbm_outs + (vmem,) * (len(outs) - hbm_outs),
        scratch_shapes=list(scratch),
        compiler_params=pltpu.CompilerParams(vmem_limit_bytes=16 * 1024 * 1024),
    )(*args)


def shape(rows, w, kind):
    return jax.ShapeDtypeStruct((rows, w), kind)


def shift(value, axis, steps):
    count = lax.axis_size(axis)
    return lax.ppermute(value, axis, [(k, (k + steps) % count) for k in range(count)])


def on_device(
    cells, halo_inputs, stale_halo, stale_returned, cotangent, expression, halo_expression,
    neighbours, edge_mask, send_rows, live_cells, ligand_genes, receptor_genes, gate_weights,
    self_weights, neighbour_weights,
):
    n, w = cells.shape[2:]
    h = halo_inputs.shape[2]
    degree = neighbours.shape[2]
    pairs = ligand_genes.shape[0]
    genes = expression.shape[3]
    b = h // 8

    vmem = pl.BlockSpec(memory_space=pltpu.VMEM)
    hbm = pl.BlockSpec(memory_space=pltpu.HBM)
    outs = (
        jax.ShapeDtypeStruct((2, 3 * b, w), BF16),
        jax.ShapeDtypeStruct((2, 3 * b, w), BF16),
        jax.ShapeDtypeStruct((2, b, w), BF16),
        jax.ShapeDtypeStruct((2, b, w), BF16),
        shape(2 * n, w, F32),
        shape(2 * n + 16, w, BF16),
        shape(8, 128, F32),
    )
    lead_m, lead_p, mid_m, mid_p, keep, send, gate = pl.pallas_call(
        tile_kernel,
        out_shape=outs,
        in_specs=[pl.BlockSpec(memory_space=pltpu.SMEM)] + [hbm] * 15,
        out_specs=(vmem,) * len(outs),
        scratch_shapes=[
            pltpu.VMEM((n + h, w), BF16),
            pltpu.VMEM((n + h, w), BF16),
            pltpu.VMEM((n + h, genes), BF16),
            pltpu.VMEM((h, w), BF16),
            pltpu.VMEM((n, w), BF16),
            pltpu.VMEM((2, w, w), BF16),
            pltpu.VMEM((2, w, w), BF16),
            pltpu.VMEM((n, n + h), BF16),
            pltpu.VMEM((n, n + h), BF16),
            pltpu.VMEM((n, n + h), F32),
            pltpu.VMEM((n, n + h), F32),
            pltpu.VMEM((n, w), F32),
            pltpu.VMEM((n, w), BF16),
            pltpu.VMEM((4 * n, w), F32),
            pltpu.VMEM((degree, n), jnp.int32),
            pltpu.VMEM((degree, n), jnp.int32),
            pltpu.VMEM((8, b), jnp.int32),
            pltpu.VMEM((1, pairs), jnp.int32),
            pltpu.VMEM((1, pairs), jnp.int32),
            pltpu.VMEM((1, pairs), F32),
            pltpu.SemaphoreType.DMA((15,)),
        ],
        compiler_params=pltpu.CompilerParams(vmem_limit_bytes=40 * 1024 * 1024),
    )(
        live_cells,
        *(
            pltpu.with_memory_space_constraint(value, pltpu.HBM)
            for value in (
                neighbours.reshape(degree, n),
                edge_mask.reshape(degree, n),
                send_rows.reshape(8, b),
                ligand_genes.reshape(1, pairs),
                receptor_genes.reshape(1, pairs),
                gate_weights.reshape(1, pairs),
                cells.reshape(n, w),
                halo_inputs.reshape(h, w),
                stale_halo.reshape(h, w),
                stale_returned.reshape(h, w),
                cotangent.reshape(n, w),
                expression.reshape(n, genes),
                halo_expression.reshape(h, genes),
                self_weights,
                neighbour_weights,
            )
        ),
    )

    def quarter(part):
        return (shape(part, w, F32), shape(8, 128, F32)) + (shape(part + 16, w, BF16),) * 3

    wide = jax.ShapeDtypeStruct((2, 3 * b, w), BF16)
    got = swap(send, "core")
    lead_m = shift(lead_m, "tx", -1)
    lead_p = shift(lead_p, "tx", 1)
    part = n // 2
    keep, gate, s1, s2, s3 = call(after_core, quarter(part), keep, gate, got)
    sends = ((1, s1), (2, s2), (3, s3))
    got = [swap(value, "first", j) for j, value in sends]
    part = part // 4
    keep, gate, s1, s2, s3, cross_m, cross_p = call(
        after_first, quarter(part) + (wide, wide), keep, gate, *got, lead_m, lead_p, mid_m, mid_p
    )
    sends = ((1, s1), (2, s2), (3, s3))
    got = [swap(value, "second", j) for j, value in sends]
    cross_m = shift(cross_m, "ty", -1)
    (both,) = call(after_second, (shape(part + 8, w, F32),), keep, gate, *got)
    (both,) = call(add_wide, (shape(part + 16, w, BF16),), both, swap(both, "z", 0))
    (both,) = call(add_narrow, (shape(part + 16, w, BF16),), both, swap(both, "z", 1))
    own, gate = call(add_last, (shape(part, w, BF16), shape(16, w, BF16)), both, swap(both, "z", 2))
    got = [swap(own, "second", j) for j in (1, 2, 3)]
    cross_p = shift(cross_p, "ty", 1)
    (own,) = call(join, (shape(4 * part, w, BF16),), own, *got)
    got = [swap(own, "first", j) for j in (1, 2, 3)]
    (own,) = call(join, (shape(16 * part + 16, w, BF16),), own, *got, gate)
    other = swap(own, "core")
    own_sq, fresh, returned = call(
        own_squares, (shape(8, w, F32), shape(h, w, BF16), shape(h, w, BF16)),
        own, lead_m, lead_p, cross_m, cross_p,
    )
    layers, gate = call(
        last_kernel, (shape(4 * n, w, F32), shape(8, 128, F32)), own, other, own_sq,
        scratch=[pltpu.VMEM((4 * n, w), F32), pltpu.SemaphoreType.DMA((8,))], hbm_outs=1,
    )
    halo_shape = (1, 1, 1, h, w)
    return (
        fresh.reshape(halo_shape),
        returned.reshape(halo_shape),
        layers.reshape(4, n, w),
        gate.reshape(pairs),
    )


def solution(mesh):
    tile = P("tx", "ty")
    return jax.shard_map(
        on_device,
        mesh=mesh,
        in_specs=(tile,) * 11 + (P(),) * 5,
        out_specs=(tile, tile, P(), P()),
        check_vma=False,
    )
```

```python
import jax
import jax.numpy as jnp
from jax import lax
from jax.experimental import pallas as pl
from jax.experimental.pallas import tpu as pltpu
from jax.sharding import PartitionSpec as P


F32 = jnp.float32
BF16 = jnp.bfloat16
AXES = ("tx", "ty")


def ring_label(position):
    return position ^ (position >> 1)


def place(index):
    tx, ty = divmod(index, 8)
    y, z_hi, core = tx // 8, (tx // 2) % 4, tx % 2
    x, z_lo = ty // 2, ty % 2
    return x, y, z_hi * 2 + z_lo, core


def index_of(x, y, z, core):
    return (y * 8 + (z // 2) * 2 + core) * 8 + x * 2 + z % 2


def unlabel(label):
    return label ^ (label >> 1)


def ring_of_eight(z, core, flip):
    spot = (z - core) % 8
    label = (spot ^ (spot >> 1)) ^ flip
    return ((label ^ (label >> 1) ^ (label >> 2)) + core) % 8


def xor_pairs(kind, flip):
    pairs = []
    for index in range(256):
        x, y, z, core = place(index)
        if kind == "core":
            core ^= 1
        elif kind == "z":
            z = ring_of_eight(z, core, (2, 4)[(flip + core) % 2])
        else:
            bit = core if kind == "first" else 1 - core
            x = unlabel(ring_label(x) ^ ((flip & 1) << bit))
            y = unlabel(ring_label(y) ^ (((flip >> 1) & 1) << bit))
            z = ring_of_eight(z, core, flip >> 2)
        pairs.append((index, index_of(x, y, z, core)))
    return pairs


def swap(value, kind, flip=1):
    return lax.ppermute(value, AXES, xor_pairs(kind, flip))


def nn(a, b):
    return lax.dot_general(a, b, (((1,), (0,)), ((), ())), preferred_element_type=F32)


def nt(a, b):
    return lax.dot_general(a, b, (((1,), (1,)), ((), ())), preferred_element_type=F32)


def tn(a, b):
    return lax.dot_general(a, b, (((0,), (0,)), ((), ())), preferred_element_type=F32)


def my_labels():
    tx, ty = lax.axis_index("tx"), lax.axis_index("ty")
    x, y, core = ring_label(ty // 2), ring_label(tx // 8), tx % 2
    low = 2 * (y & 1) + (x & 1)
    high = 2 * (y >> 1) + (x >> 1)
    mine = jnp.where(core == 0, high, low)
    partner = jnp.where(core == 0, low, high)
    return core, mine, partner


def put_gate(ref, row, gate):
    hi = gate.astype(BF16).astype(F32)
    lo = (gate - hi).astype(BF16).astype(F32)
    ref[row : row + 16, 0:128] = jnp.concatenate([hi, lo], 0).astype(BF16)
    return hi + lo


def get_gate(ref, row):
    both = ref[row : row + 16, 0:128].astype(F32)
    return both[0:8] + both[8:16]


def tile_kernel(
    live_ref, nbr_in, msk_in, snd_in, lig_in, rec_in, gwt_in,
    cells, halo, stale, sback, cot, expr, hexpr, ws, wn,
    o_lm, o_lp, o_mm, o_mp, o_keep, o_send, o_gate,
    full0, full1, xall, sb, ct, wsv, wnv, cnt, adj, slope_g, inner, slope0, agg0, grads,
    nbr, msk, snd, lig, rec, gwt, sems,
):
    n, w = ct.shape
    full_n = full0.shape[0]

    def fetch(src, dst, slot):
        copy = pltpu.make_async_copy(src, dst, sems.at[slot])
        copy.start()
        return copy

    small = (
        (nbr_in, nbr), (msk_in, msk), (lig_in, lig), (rec_in, rec), (gwt_in, gwt), (snd_in, snd),
    )
    c_small = [fetch(src, dst, 9 + k) for k, (src, dst) in enumerate(small)]
    c_expr = fetch(expr, xall.at[pl.ds(0, n)], 0)
    c_hexpr = fetch(hexpr, xall.at[pl.ds(n, full_n - n)], 1)
    c_cells = fetch(cells, full0.at[pl.ds(0, n)], 2)
    c_halo = fetch(halo, full0.at[pl.ds(n, full_n - n)], 3)
    c_ws = fetch(ws, wsv, 4)
    c_wn = fetch(wn, wnv, 5)
    c_stale = fetch(stale, full1.at[pl.ds(n, full_n - n)], 6)
    c_cot = fetch(cot, ct, 7)
    c_sb = fetch(sback, sb, 8)

    for copy in c_small:
        copy.wait()
    ids = nbr[...]
    low = jnp.bitwise_and(ids, 127)
    field = jnp.left_shift(msk[...], 5 * jnp.right_shift(ids, 7))
    rows128 = lax.broadcasted_iota(jnp.int32, (128, 128), 0)
    for part in range(n // 128):
        cols = slice(part * 128, part * 128 + 128)
        words = jnp.zeros((128, 128), jnp.int32)
        for k in range(ids.shape[0]):
            words = words + jnp.where(rows128 == low[k : k + 1, cols], field[k : k + 1, cols], 0)
        words = words.T
        for block in range(full_n // 128):
            count = jnp.bitwise_and(jnp.right_shift(words, 5 * block), 31)
            cnt[cols, block * 128 : block * 128 + 128] = (0.25 * count.astype(F32)).astype(BF16)

    genes = xall.shape[1]
    pairs = lig.shape[1]
    gene_rows = lax.broadcasted_iota(jnp.int32, (genes, pairs), 0)
    rec_table = jnp.where(gene_rows == rec[...], gwt[...], 0.0).astype(BF16)
    lig_table = jnp.where(gene_rows == lig[...], 1.0, 0.0).astype(BF16)
    mixed = nt(rec_table, lig_table).astype(BF16)
    c_expr.wait()
    c_hexpr.wait()
    left = nn(xall[0:n], mixed).astype(BF16)
    half_tanh = 0.5 * jnp.tanh(0.5 * nt(left, xall[...]))
    count = cnt[...].astype(F32)
    weight = count * (0.5 + half_tanh)
    adj[...] = weight.astype(BF16)
    slope_g[...] = weight * (0.5 - half_tanh)

    c_cells.wait()
    c_halo.wait()
    state0 = full0[0:n]
    agg0[...] = nn(adj[...], full0[...]).astype(BF16)
    c_ws.wait()
    c_wn.wait()
    pre0 = nn(state0, wsv[0]) + nn(agg0[...], wnv[0])
    sig0 = 0.5 + 0.5 * jnp.tanh(0.5 * pre0)
    slope0[...] = sig0 * (1.0 + pre0 * (1.0 - sig0))
    full1[0:n] = (state0.astype(F32) + pre0 * sig0).astype(BF16)

    c_stale.wait()
    agg1 = nn(adj[...], full1[...]).astype(BF16)
    pre1 = nn(full1[0:n], wsv[1]) + nn(agg1, wnv[1])
    sig1 = 0.5 + 0.5 * jnp.tanh(0.5 * pre1)
    slope1 = sig1 * (1.0 + pre1 * (1.0 - sig1))
    c_cot.wait()
    live = lax.broadcasted_iota(jnp.int32, (n, w), 0) < live_ref[0, 0]
    carried = jnp.where(live, ct[...].astype(F32), 0.0)
    gpre1 = (carried * slope1).astype(BF16)
    grads[2 * n : 3 * n] = tn(full1[0:n], gpre1)
    grads[3 * n : 4 * n] = tn(agg1, gpre1)
    gagg1 = nt(gpre1, wnv[1]).astype(BF16)
    inner[...] = nt(gagg1, full1[...])
    gfull = tn(adj[...], gagg1)
    back = gfull[n:].astype(BF16)

    send_ids = jnp.concatenate([snd[d : d + 1] for d in range(8)], axis=1)
    sent = send_ids.shape[1]
    send_table = jnp.where(
        lax.broadcasted_iota(jnp.int32, (n, sent), 0) == send_ids, 1.0, 0.0
    ).astype(BF16)
    fresh = tn(send_table, full1[0:n]).astype(BF16)
    b = sent // 8
    o_lm[0] = fresh[0 : 3 * b]
    o_lp[0] = fresh[5 * b : 8 * b]
    o_mm[0] = fresh[3 * b : 4 * b]
    o_mp[0] = fresh[4 * b : 5 * b]
    for pos in range(3):
        o_lm[1, pos * b : (pos + 1) * b] = back[(7 - pos) * b : (8 - pos) * b]
        o_lp[1, pos * b : (pos + 1) * b] = back[(2 - pos) * b : (3 - pos) * b]
    o_mm[1] = back[4 * b : 5 * b]
    o_mp[1] = back[3 * b : 4 * b]

    c_sb.wait()
    carried = carried + nt(gpre1, wsv[1]) + gfull[:n] + nn(send_table, sb[...])
    gpre0 = (carried * slope0[...]).astype(BF16)
    grads[0:n] = tn(state0, gpre0)
    grads[n : 2 * n] = tn(agg0[...], gpre0)
    gagg0 = nt(gpre0, wnv[0]).astype(BF16)
    spread = (slope_g[...] * (inner[...] + nt(gagg0, full0[...]))).astype(BF16)
    gathered = nn(spread, xall[...]).astype(BF16)
    gene_grad = tn(xall[0:n], gathered)
    gene_hi = gene_grad.astype(BF16)
    gene_lo = (gene_grad - gene_hi.astype(F32)).astype(BF16)
    by_pair = nn(gene_hi, lig_table) + nn(gene_lo, lig_table)
    gate = jnp.sum(jnp.where(gene_rows == rec[...], by_pair, 0.0), axis=0, keepdims=True)
    gate = jnp.concatenate([gate[:, k * 128 : k * 128 + 128] for k in range(8)], axis=0)

    core, mine, partner = my_labels()
    half = 2 * n
    step = half // 32
    for j in range(32):
        here = pl.multiple_of(core * half + (mine ^ j) * step, step)
        there = pl.multiple_of((1 - core) * half + (partner ^ j) * step, step)
        o_keep[j * step : (j + 1) * step] = grads[pl.ds(here, step)]
        o_send[j * step : (j + 1) * step] = grads[pl.ds(there, step)].astype(BF16)
    o_gate[...] = put_gate(o_send, half, gate)


def split(total, gates, rows, keep, gate_out, sends):
    part = rows // (len(sends) + 1)
    keep[...] = total(0, part)
    for j, ref in enumerate(sends, 1):
        ref[0:part] = total(j * part, (j + 1) * part).astype(BF16)
        kept = put_gate(ref, part, gates)
    gate_out[...] = kept


def put_valid(dst, src, valid):
    @pl.when(valid)
    def _():
        dst[...] = src[...]

    @pl.when(jnp.logical_not(valid))
    def _():
        dst[...] = jnp.zeros(dst.shape, dst.dtype)


def has_after(axis):
    return lax.axis_index(axis) < lax.axis_size(axis) - 1


def has_before(axis):
    return lax.axis_index(axis) > 0


def tree(values):
    while len(values) > 1:
        values = [values[k] + values[k + 1] for k in range(0, len(values), 2)]
    return values[0]


def summed(own, got):
    return lambda lo, hi: tree([own[lo:hi]] + [ref[lo:hi].astype(F32) for ref in got])


def summed_gates(gate, got, rows):
    return tree([gate[...]] + [get_gate(ref, rows) for ref in got])


def after_core(own, gate, got, out):
    members, rows = out.shape[0], out.shape[1] - 16
    gates = gate[...] + get_gate(got, own.shape[0])
    for p in range(members):
        cut = slice(p * rows, (p + 1) * rows)
        out[p, 0:rows] = (own[cut] + got[cut].astype(F32)).astype(BF16)
        put_gate(out.at[p], rows, gates)


def after_first(
    got, lead_m, lead_p, mid_m, mid_p, keep, gate_out, s1, s2, s3, cross_m, cross_p,
):
    members, rows = got.shape[0], got.shape[1] - 16
    gates = tree([get_gate(got.at[p], rows) for p in range(members)])

    def total(lo, hi):
        return tree([got[p, lo:hi].astype(F32) for p in range(members)])

    split(total, gates, rows, keep, gate_out, (s1, s2, s3))
    b = mid_m.shape[1]
    for k in range(2):
        for ref, mid, cut in ((cross_m, mid_m, 0), (cross_p, mid_p, 2)):
            ref[k, 0:b] = mid[k]
            rows = pl.ds(cut * b, b)
            put_valid(ref.at[k, pl.ds(b, b)], lead_m.at[k, rows], has_after("tx"))
            put_valid(ref.at[k, pl.ds(2 * b, b)], lead_p.at[k, rows], has_before("tx"))


def after_second(own, gate, r1, r2, r3, out):
    rows = own.shape[0]
    got = (r1, r2, r3)
    out[0:rows] = summed(own, got)(0, rows).astype(BF16)
    put_gate(out, rows, summed_gates(gate, got, rows))


def add_narrow(a, b, out):
    rows = out.shape[0] - 16
    out[0:rows] = (a[0:rows].astype(F32) + b[0:rows].astype(F32)).astype(BF16)
    put_gate(out, rows, get_gate(a, rows) + get_gate(b, rows))


def add_last(a, b, own, gate):
    rows = own.shape[0]
    own[...] = (a[0:rows].astype(F32) + b[0:rows].astype(F32)).astype(BF16)
    put_gate(gate, 0, get_gate(a, rows) + get_gate(b, rows))


def join(own, r1, r2, r3, gate, out):
    for p in range(out.shape[0]):
        row = 0
        for ref in (own, r1, r2, r3, gate):
            out[p, row : row + ref.shape[0]] = ref[...]
            row += ref.shape[0]


def squares(ref, label):
    members, rows, w = ref.shape[0], ref.shape[1] - 16, ref.shape[2]
    step = rows // 4
    total = jnp.zeros((8, w), F32)
    for p in range(members):
        for j in range(4):
            row = pl.multiple_of((label ^ j) * step, step)
            part = ref[p, pl.ds(row, step)].astype(F32)
            part = part * part
            for k in range(step // 8):
                total = total + part[k * 8 : (k + 1) * 8]
    return total


def own_squares(own, lead_m, lead_p, cross_m, cross_p, o_squares, o_fresh, o_returned):
    _, mine, _ = my_labels()
    o_squares[...] = squares(own, mine)
    b = o_fresh.shape[0] // 8
    l_m, l_p = (lead_m, has_after("tx")), (lead_p, has_before("tx"))
    c_m, c_p = (cross_m, has_after("ty")), (cross_p, has_before("ty"))
    arrived = (
        (c_m, 1), (l_m, 1), (c_p, 1), (c_m, 0), (c_p, 0), (c_m, 2), (l_p, 1), (c_p, 2),
    )
    for d, ((ref, valid), cut) in enumerate(arrived):
        rows = pl.ds(cut * b, b)
        put_valid(o_fresh.at[pl.ds(d * b, b)], ref.at[0, rows], valid)
        put_valid(o_returned.at[pl.ds((7 - d) * b, b)], ref.at[1, rows], valid)


def last_kernel(own, other, own_sq, o_layers, o_gate, whole, sems):
    members, rows, w = own.shape[0], own.shape[1] - 16, own.shape[2]
    core, mine, partner = my_labels()
    step = rows // 4
    other_sq = squares(other, partner)
    gate = jnp.where(core == 0, get_gate(own.at[0], rows), get_gate(other.at[0], rows))
    total = jnp.sum(own_sq[...] + other_sq, axis=0, keepdims=True)
    square = jnp.sum(total, axis=1, keepdims=True)
    square = square + jnp.sum(
        jnp.sum(gate * gate, axis=0, keepdims=True), axis=1, keepdims=True
    )
    clip = jnp.minimum(1.0, (2.0 * w) / jnp.sqrt(square + 1e-06))
    o_gate[...] = gate * clip
    copies = []
    for side, (ref, label, which) in enumerate(((own, mine, core), (other, partner, 1 - core))):
        for p in range(members):
            base = (side * members + p) * rows
            for j in range(4):
                row = pl.multiple_of((label ^ j) * step, step)
                part = ref[p, pl.ds(row, step)].astype(F32) * clip
                whole[base + j * step : base + (j + 1) * step] = part
            target = pl.multiple_of(which * (members * rows) + p * rows, rows)
            copy = pltpu.make_async_copy(
                whole.at[pl.ds(base, rows)],
                o_layers.at[pl.ds(target, rows)],
                sems.at[side * members + p],
            )
            copy.start()
            copies.append(copy)
    for copy in copies:
        copy.wait()


def call(kernel, outs, *args, scratch=(), hbm_outs=0):
    vmem, hbm = pl.BlockSpec(memory_space=pltpu.VMEM), pl.BlockSpec(memory_space=pl.ANY)
    return pl.pallas_call(
        kernel,
        out_shape=outs,
        in_specs=[vmem] * len(args),
        out_specs=(hbm,) * hbm_outs + (vmem,) * (len(outs) - hbm_outs),
        scratch_shapes=list(scratch),
        compiler_params=pltpu.CompilerParams(vmem_limit_bytes=16 * 1024 * 1024),
    )(*args)


def shape(rows, w, kind):
    return jax.ShapeDtypeStruct((rows, w), kind)


def groups_of_eight():
    groups = {}
    for index in range(256):
        x, y, z, core = place(index)
        spot = (z - core) % 8
        bit = ring_label(x) >> core & 1, ring_label(y) >> core & 1, (spot ^ (spot >> 1)) & 1
        first = bit[0] + 2 * bit[1] + 4 * bit[2]
        others = [dict(xor_pairs("first", j))[index] for j in range(8)]
        groups.setdefault(min(others), {})[first] = index
    return [[group[k] for k in range(8)] for _, group in sorted(groups.items())]


def exchange(value):
    return lax.all_to_all(
        value, AXES, 0, 0, axis_index_groups=groups_of_eight(), tiled=True
    )


def shift(value, axis, steps):
    count = lax.axis_size(axis)
    return lax.ppermute(value, axis, [(k, (k + steps) % count) for k in range(count)])


def on_device(
    cells, halo_inputs, stale_halo, stale_returned, cotangent, expression, halo_expression,
    neighbours, edge_mask, send_rows, live_cells, ligand_genes, receptor_genes, gate_weights,
    self_weights, neighbour_weights,
):
    n, w = cells.shape[2:]
    h = halo_inputs.shape[2]
    degree = neighbours.shape[2]
    pairs = ligand_genes.shape[0]
    genes = expression.shape[3]
    b = h // 8

    vmem = pl.BlockSpec(memory_space=pltpu.VMEM)
    hbm = pl.BlockSpec(memory_space=pltpu.HBM)
    outs = (
        jax.ShapeDtypeStruct((2, 3 * b, w), BF16),
        jax.ShapeDtypeStruct((2, 3 * b, w), BF16),
        jax.ShapeDtypeStruct((2, b, w), BF16),
        jax.ShapeDtypeStruct((2, b, w), BF16),
        shape(2 * n, w, F32),
        shape(2 * n + 16, w, BF16),
        shape(8, 128, F32),
    )
    lead_m, lead_p, mid_m, mid_p, keep, send, gate = pl.pallas_call(
        tile_kernel,
        out_shape=outs,
        in_specs=[pl.BlockSpec(memory_space=pltpu.SMEM)] + [hbm] * 15,
        out_specs=(vmem,) * len(outs),
        scratch_shapes=[
            pltpu.VMEM((n + h, w), BF16),
            pltpu.VMEM((n + h, w), BF16),
            pltpu.VMEM((n + h, genes), BF16),
            pltpu.VMEM((h, w), BF16),
            pltpu.VMEM((n, w), BF16),
            pltpu.VMEM((2, w, w), BF16),
            pltpu.VMEM((2, w, w), BF16),
            pltpu.VMEM((n, n + h), BF16),
            pltpu.VMEM((n, n + h), BF16),
            pltpu.VMEM((n, n + h), F32),
            pltpu.VMEM((n, n + h), F32),
            pltpu.VMEM((n, w), F32),
            pltpu.VMEM((n, w), BF16),
            pltpu.VMEM((4 * n, w), F32),
            pltpu.VMEM((degree, n), jnp.int32),
            pltpu.VMEM((degree, n), jnp.int32),
            pltpu.VMEM((8, b), jnp.int32),
            pltpu.VMEM((1, pairs), jnp.int32),
            pltpu.VMEM((1, pairs), jnp.int32),
            pltpu.VMEM((1, pairs), F32),
            pltpu.SemaphoreType.DMA((15,)),
        ],
        compiler_params=pltpu.CompilerParams(vmem_limit_bytes=40 * 1024 * 1024),
    )(
        live_cells,
        *(
            pltpu.with_memory_space_constraint(value, pltpu.HBM)
            for value in (
                neighbours.reshape(degree, n),
                edge_mask.reshape(degree, n),
                send_rows.reshape(8, b),
                ligand_genes.reshape(1, pairs),
                receptor_genes.reshape(1, pairs),
                gate_weights.reshape(1, pairs),
                cells.reshape(n, w),
                halo_inputs.reshape(h, w),
                stale_halo.reshape(h, w),
                stale_returned.reshape(h, w),
                cotangent.reshape(n, w),
                expression.reshape(n, genes),
                halo_expression.reshape(h, genes),
                self_weights,
                neighbour_weights,
            )
        ),
    )

    def parts(part, sends):
        return (shape(part, w, F32), shape(8, 128, F32)) + (shape(part + 16, w, BF16),) * sends

    wide = jax.ShapeDtypeStruct((2, 3 * b, w), BF16)
    got = swap(send, "core")
    lead_m = shift(lead_m, "tx", -1)
    lead_p = shift(lead_p, "tx", 1)
    eight = jax.ShapeDtypeStruct((8, n // 4 + 16, w), BF16)
    (eighths,) = call(after_core, (eight,), keep, gate, got)
    got = exchange(eighths)
    part = n // 16
    keep, gate, *sends, cross_m, cross_p = call(
        after_first, parts(part, 3) + (wide, wide), got, lead_m, lead_p, mid_m, mid_p
    )
    got = [swap(value, "second", j) for j, value in enumerate(sends, 1)]
    cross_m = shift(cross_m, "ty", -1)
    narrow = (shape(part + 16, w, BF16),)
    (both,) = call(after_second, narrow, keep, gate, *got)
    (both,) = call(add_narrow, narrow, both, swap(both, "z", 0))
    own, gate = call(add_last, (shape(part, w, BF16), shape(16, w, BF16)), both, swap(both, "z", 1))
    got = [swap(own, "second", j) for j in range(1, 4)]
    cross_p = shift(cross_p, "ty", 1)
    (own,) = call(join, (eight,), own, *got, gate)
    own = exchange(own)
    other = swap(own, "core")
    own_sq, fresh, returned = call(
        own_squares, (shape(8, w, F32), shape(h, w, BF16), shape(h, w, BF16)),
        own, lead_m, lead_p, cross_m, cross_p,
    )
    layers, gate = call(
        last_kernel, (shape(4 * n, w, F32), shape(8, 128, F32)), own, other, own_sq,
        scratch=[pltpu.VMEM((4 * n, w), F32), pltpu.SemaphoreType.DMA((16,))], hbm_outs=1,
    )
    halo_shape = (1, 1, 1, h, w)
    return (
        fresh.reshape(halo_shape),
        returned.reshape(halo_shape),
        layers.reshape(4, n, w),
        gate.reshape(pairs),
    )


def solution(mesh):
    tile = P("tx", "ty")
    return jax.shard_map(
        on_device,
        mesh=mesh,
        in_specs=(tile,) * 11 + (P(),) * 5,
        out_specs=(tile, tile, P(), P()),
        check_vma=False,
    )
```
